32 devices in a mesh: gz: 16 (over z, y, x), gy: 2 (over core).
Axes of the slice: x: 2, y: 2, z: 4, core: 2. Of those that a mesh axis runs over, the one named last changes fastest.
Arguments:
- fodf: float32 [192, 16, 32, 128], P(None, 'gy', 'gz'), may hold values from 0 to 21, as said below
- directions: float32 [3, 192], replicated, may hold values from -1 to 1, as said below
- signs: int32 [3, 192], replicated, may hold values from -1 to 1, as said below
Outputs:
- enhanced: float32 [192, 16, 32, 128], P(None, 'gy', 'gz')
The draws below stay inside these ranges and needn't reach their ends.
Inputs may be any that keep to these rules, and one draw needn't show every extreme that they name: `fodf`: Non-negative densities. `directions`: unit vectors; orientation k + 96 is the antipode of orientation k; no component is zero. `signs`: each sign is the sign of the matching component of directions; along each axis exactly 96 orientations have sign 1.
All inputs are finite; a program needn't handle non-finite values.
Results may differ from the reference program's by a relative error of at most 0.0003.
Values sent between devices are 32-bit elements; how exact they have to be, the bound alone decides.
No kernel may reach another device: no remote copies, remote signals or barrier semaphores. Data moves between devices by JAX's collectives and lax.ppermute only.
A program may use at most 64 MiB of HBM per device.

```python
import math
import jax
import jax.numpy as jnp
from jax import lax

K = 192
LMAX = 8
X = 128
ITERS = 4
NY = 16
NZ = 32


def orientation_pairs(key):
    halves = K // 2
    signs_half = 2 * jax.random.randint(jax.random.fold_in(key, 17), (3, halves), 0, 2) - 1
    magnitude = jax.random.uniform(jax.random.fold_in(key, 29), (3, halves), jnp.float32, 0.15, 1.0)
    vectors = signs_half.astype(jnp.float32) * magnitude
    vectors = vectors / jnp.sqrt(jnp.sum(vectors * vectors, axis=0, keepdims=True))
    return (jnp.concatenate([vectors, -vectors], 1), jnp.concatenate([signs_half, -signs_half], 1).astype(jnp.int32))


def draw_directions(key, part):
    return orientation_pairs(key)[0]


def draw_signs(key, part):
    return orientation_pairs(key)[1]


def draw_fodf(key, part):
    grid_shape = (K, NY, NZ, X)
    normal_part = jnp.clip(jax.random.normal(jax.random.fold_in(key, 5), grid_shape, jnp.float32), -5.0, 5.0)
    return jnp.exp(0.6 * normal_part)


def setup_inputs(seed: int = 0) -> dict:
    key_list = jax.random.split(jax.random.key(seed), 4)
    return {
        "fodf": draw_fodf(jax.random.fold_in(key_list[3], 71), 0),
        "directions": draw_directions(jax.random.fold_in(key_list[3], 71), 0),
        "signs": draw_signs(jax.random.fold_in(key_list[3], 71), 0),
    }


TIME_STEP = 0.5
DIFFUSION = 0.02

def double_factorial(value):
    result = 1
    while value > 1:
        result = result * value
        value = value - 2
    return result

def harmonic_rows(directions):
    along_x, along_y, along_z = (directions[0], directions[1], directions[2])
    cosines = [jnp.ones_like(along_x)]
    sines = [jnp.zeros_like(along_x)]
    for order in range(1, LMAX + 1):
        cosines.append(cosines[-1] * along_x - sines[-1] * along_y)
        sines.append(cosines[-2] * along_y + sines[-1] * along_x)
    legendre = {}
    for order in range(LMAX + 1):
        legendre[order, order] = double_factorial(2 * order - 1) * jnp.ones_like(along_z)
        if order + 1 <= LMAX:
            legendre[order + 1, order] = (2 * order + 1) * along_z * legendre[order, order]
        for degree in range(order + 2, LMAX + 1):
            legendre[degree, order] = ((2 * degree - 1) * along_z * legendre[degree - 1, order] - (degree + order - 1) * legendre[degree - 2, order]) / (degree - order)
    basis_rows = []
    eigen_values = []
    for degree in range(0, LMAX + 1, 2):
        for order in range(degree + 1):
            weight_norm = math.sqrt((2 * degree + 1) * math.factorial(degree - order) / math.factorial(degree + order))
            basis_rows.append(weight_norm * legendre[degree, order] * cosines[order])
            eigen_values.append(-float(degree * (degree + 1)))
            if order > 0:
                basis_rows.append(weight_norm * legendre[degree, order] * sines[order])
                eigen_values.append(-float(degree * (degree + 1)))
    return (jnp.stack(basis_rows, 0), jnp.array(eigen_values, dtype=directions.dtype))

def angular_maps(directions):
    basis, eigen_values = harmonic_rows(directions)
    gram = jnp.dot(basis, basis.T, precision=lax.Precision.HIGHEST)
    chol_lower = jnp.linalg.cholesky(gram)
    partial_solve = lax.linalg.triangular_solve(chol_lower, basis, left_side=True, lower=True)
    analysis = lax.linalg.triangular_solve(chol_lower, partial_solve, left_side=True, lower=True, transpose_a=True)
    synthesis = basis.T * eigen_values[None, :]
    return (analysis, synthesis)

def reference(fodf, directions, signs):
    analysis, synthesis = angular_maps(directions)
    speeds = jnp.abs(directions).T
    upwinds = signs.T
    field = fodf
    for sweep in range(ITERS):
        coeffs = jnp.dot(analysis, field.reshape(K, -1), precision=lax.Precision.HIGHEST)

        def single(items):
            row, speed_row, upwind_row, synth_row = items
            padded = jnp.pad(row, 1)
            center = row
            pairs = [(padded[1:-1, 1:-1, :-2], padded[1:-1, 1:-1, 2:]), (padded[:-2, 1:-1, 1:-1], padded[2:, 1:-1, 1:-1]), (padded[1:-1, :-2, 1:-1], padded[1:-1, 2:, 1:-1])]
            transport = jnp.zeros_like(center)
            for axis_number in range(3):
                beneath, beyond = pairs[axis_number]
                chosen = jnp.where(upwind_row[axis_number] > 0, beneath, beyond)
                transport = transport + speed_row[axis_number] * (center - chosen)
            angular = jnp.dot(synth_row, coeffs, precision=lax.Precision.HIGHEST).reshape(row.shape)
            return center - TIME_STEP * transport + TIME_STEP * DIFFUSION * angular
        field = lax.map(single, (field, speeds, upwinds, synthesis))
    return field
```

```python
import functools
import math

import jax
import jax.numpy as jnp
from jax import lax
from jax.experimental import pallas as pl
from jax.experimental.pallas import tpu as pltpu
from jax.sharding import PartitionSpec as P

LMAX = 8
ITERS = 4
TIME_STEP = 0.5
DIFFUSION = 0.02

VMEM = pltpu.VMEM
SMEM = pltpu.SMEM


def double_factorial(value):
    result = 1
    while value > 1:
        result = result * value
        value = value - 2
    return result


def harmonic_rows(directions):
    along_x, along_y, along_z = (directions[0], directions[1], directions[2])
    cosines = [jnp.ones_like(along_x)]
    sines = [jnp.zeros_like(along_x)]
    for order in range(1, LMAX + 1):
        cosines.append(cosines[-1] * along_x - sines[-1] * along_y)
        sines.append(cosines[-2] * along_y + sines[-1] * along_x)
    legendre = {}
    for order in range(LMAX + 1):
        legendre[order, order] = double_factorial(2 * order - 1) * jnp.ones_like(along_z)
        if order + 1 <= LMAX:
            legendre[order + 1, order] = (2 * order + 1) * along_z * legendre[order, order]
        for degree in range(order + 2, LMAX + 1):
            legendre[degree, order] = (
                (2 * degree - 1) * along_z * legendre[degree - 1, order]
                - (degree + order - 1) * legendre[degree - 2, order]
            ) / (degree - order)
    basis_rows = []
    eigen_values = []
    for degree in range(0, LMAX + 1, 2):
        for order in range(degree + 1):
            weight_norm = math.sqrt(
                (2 * degree + 1) * math.factorial(degree - order) / math.factorial(degree + order)
            )
            basis_rows.append(weight_norm * legendre[degree, order] * cosines[order])
            eigen_values.append(-float(degree * (degree + 1)))
            if order > 0:
                basis_rows.append(weight_norm * legendre[degree, order] * sines[order])
                eigen_values.append(-float(degree * (degree + 1)))
    return (jnp.stack(basis_rows, 0), jnp.array(eigen_values, dtype=directions.dtype))


def angular_matrix(half):
    basis, eigen_values = harmonic_rows(half)
    gram = 2.0 * jnp.dot(basis, basis.T, precision=lax.Precision.HIGHEST)
    chol_lower = jnp.linalg.cholesky(gram)
    partial_solve = lax.linalg.triangular_solve(chol_lower, basis, left_side=True, lower=True)
    analysis = lax.linalg.triangular_solve(
        chol_lower, partial_solve, left_side=True, lower=True, transpose_a=True
    )
    synthesis = basis.T * (TIME_STEP * DIFFUSION * eigen_values)[None, :]
    return jnp.dot(synthesis, analysis, precision=lax.Precision.HIGHEST)


def exchange(even_load, odd_load, axis):
    peers = lax.axis_size(axis)
    first = [(i, i ^ 1) for i in range(peers)]
    second = [(i, i + 1 if i % 2 else i - 1) for i in range(1, peers - 1)]
    got = [lax.ppermute(even_load, axis, first)]
    if second:
        got.append(lax.ppermute(odd_load, axis, second))
    return got


class Plan:
    def __init__(self, shape, z_peers, y_peers):
        self.kk, self.ny, self.nz, self.nx = shape
        self.half = self.kk // 2
        self.rows = self.ny * self.nz
        self.z_two = z_peers > 2
        self.y_two = y_peers > 2
        self.layer = jax.ShapeDtypeStruct((self.ny, self.half, self.nx), jnp.float32)
        self.rest = jax.ShapeDtypeStruct((2, self.nz - 1, self.ny, self.half, self.nx), jnp.float32)
        self.edge = jax.ShapeDtypeStruct((self.nz, self.half, self.nx), jnp.float32)
        self.field = jax.ShapeDtypeStruct((self.kk * self.rows, self.nx), jnp.float32)


def column(table, index, shape):
    return jnp.broadcast_to(table[:, index : index + 1], shape)


def from_below(even, got):
    first = got[0]
    if len(got) == 1:
        return jnp.where(even, jnp.zeros_like(first), first)
    return jnp.where(even, got[1], first)


def from_above(even, got):
    first = got[0]
    if len(got) == 1:
        return jnp.where(even, first, jnp.zeros_like(first))
    return jnp.where(even, first, got[1])


def write_edges(even, rising_y, get_p, get_n, plan, outs):
    for z in range(plan.nz):
        top, low = plan.ny - 1, 0
        up = jnp.where(rising_y, get_p(z, top), get_n(z, top))
        down = jnp.where(rising_y, get_n(z, low), get_p(z, low))
        outs[0][z] = jnp.where(even, up, down)
        if plan.y_two:
            outs[1][z] = jnp.where(even, down, up)


def open_body(plan, flags, table, field, even_ref, odd_ref, rest_ref, *edges):
    shape = (plan.half, plan.nx)
    even = flags[0] == 0
    rising_z = column(table, 6, shape) > 0
    rising_y = column(table, 5, shape) > 0
    kept = {}
    for y in range(plan.ny):
        for z in range(plan.nz):
            row = y * plan.nz + z
            a = field[pl.ds(row, plan.half, stride=plan.rows), :]
            b = field[pl.ds(row + plan.half * plan.rows, plan.half, stride=plan.rows), :]
            p = jnp.where(rising_z, a, b)
            n = jnp.where(rising_z, b, a)
            if z < plan.nz - 1:
                rest_ref[0, z, y] = p
            if z > 0:
                rest_ref[1, z - 1, y] = n
            if z == plan.nz - 1:

                @pl.when(even)
                def _():
                    even_ref[y] = p

                @pl.when(jnp.logical_not(even))
                def _():
                    odd_ref[y] = p

            if z == 0:

                @pl.when(even)
                def _():
                    odd_ref[y] = n

                @pl.when(jnp.logical_not(even))
                def _():
                    even_ref[y] = n

            if y in (0, plan.ny - 1):
                kept[z, y] = (p, n)
    write_edges(
        flags[1] == 0,
        rising_y,
        lambda z, y: kept[z, y][0],
        lambda z, y: kept[z, y][1],
        plan,
        edges,
    )


def member_reader(plan, even, state, got, speed_z):
    even_ref, odd_ref, rest_ref = state

    def get_p(z, y):
        if z == plan.nz - 1:
            return jnp.where(even, even_ref[y], odd_ref[y])
        value = rest_ref[0, z, y]
        if got is not None and z == 0:
            value = value + speed_z * from_below(even, [g[y] for g in got])
        return value

    def get_n(z, y):
        if z == 0:
            return jnp.where(even, odd_ref[y], even_ref[y])
        value = rest_ref[1, z - 1, y]
        if got is not None and z == plan.nz - 1:
            value = value + speed_z * from_above(even, [g[y] for g in got])
        return value

    return get_p, get_n


def edge_body(plan, flags, table, even_ref, odd_ref, rest_ref, *refs):
    count = 1 + plan.z_two
    got, edges = refs[:count], refs[count:]
    shape = (plan.half, plan.nx)
    get_p, get_n = member_reader(
        plan, flags[0] == 0, (even_ref, odd_ref, rest_ref), got, column(table, 3, shape)
    )
    write_edges(flags[1] == 0, column(table, 5, shape) > 0, get_p, get_n, plan, edges)


def step_body(plan, first, flags, table, matrix, even_ref, odd_ref, rest_ref, *refs):
    z_count = 0 if first else 1 + plan.z_two
    y_count = 1 + plan.y_two
    got = None if first else refs[:z_count]
    y_got = refs[z_count : z_count + y_count]
    new_even, new_odd, new_rest, full, sums, turn = refs[z_count + y_count :]
    half, nx, ny, nz = plan.half, plan.nx, plan.ny, plan.nz
    shape = (half, nx)
    even = flags[0] == 0
    y_even = flags[1] == 0
    get_p, get_n = member_reader(
        plan, even, (even_ref, odd_ref, rest_ref), got, column(table, 3, shape)
    )
    for z in range(nz):
        low = from_below(y_even, [g[z] for g in y_got])
        high = from_above(y_even, [g[z] for g in y_got])
        full[0, z, 0] = low
        full[1, z, 0] = low
        full[0, z, ny + 1] = high
        full[1, z, ny + 1] = high
        for y in range(ny):
            p = get_p(z, y)
            n = get_n(z, y)
            full[0, z, y + 1] = p
            full[1, z, y + 1] = n
            row = z * ny + y
            sums[:, row * nx : (row + 1) * nx] = p + n
    turn[...] = jnp.dot(
        matrix[...],
        sums[...],
        precision=lax.Precision.HIGHEST,
        preferred_element_type=jnp.float32,
    )
    lane = lax.broadcasted_iota(jnp.int32, (8, nx), 1)
    first_lane = lane == 0
    last_lane = lane == nx - 1
    for part in range(half // 8):
        rows = pl.ds(part * 8, 8)
        tab = table[rows, :]
        tile = (8, nx)
        rest_speed = column(tab, 0, tile)
        speed_x = column(tab, 1, tile)
        speed_y = column(tab, 2, tile)
        speed_z = column(tab, 3, tile)
        rising_x = column(tab, 4, tile) > 0
        rising_y = column(tab, 5, tile) > 0
        for z in range(nz):
            for y in range(ny):
                row = z * ny + y
                p = full[0, z, y + 1, rows, :]
                n = full[1, z, y + 1, rows, :]
                u = jnp.where(rising_x, p, n)
                v = jnp.where(rising_x, n, p)
                u = jnp.where(first_lane, 0.0, pltpu.roll(u, 1, 1))
                v = jnp.where(last_lane, 0.0, pltpu.roll(v, nx - 1, 1))
                angular = turn[rows, row * nx : (row + 1) * nx]
                new_p = rest_speed * p + speed_x * jnp.where(rising_x, u, v) + angular
                new_n = rest_speed * n + speed_x * jnp.where(rising_x, v, u) + angular
                new_p = new_p + speed_y * jnp.where(
                    rising_y, full[0, z, y, rows, :], full[0, z, y + 2, rows, :]
                )
                new_n = new_n + speed_y * jnp.where(
                    rising_y, full[1, z, y + 2, rows, :], full[1, z, y, rows, :]
                )
                if z > 0:
                    new_p = new_p + speed_z * full[0, z - 1, y + 1, rows, :]
                if z < nz - 1:
                    new_n = new_n + speed_z * full[1, z + 1, y + 1, rows, :]
                if z < nz - 1:
                    new_rest[0, z, y, rows, :] = new_p
                if z > 0:
                    new_rest[1, z - 1, y, rows, :] = new_n
                if z == nz - 1:
                    full_p = new_p

                    @pl.when(even)
                    def _():
                        new_even[y, rows, :] = full_p

                    @pl.when(jnp.logical_not(even))
                    def _():
                        new_odd[y, rows, :] = full_p

                if z == 0:
                    full_n = new_n

                    @pl.when(even)
                    def _():
                        new_odd[y, rows, :] = full_n

                    @pl.when(jnp.logical_not(even))
                    def _():
                        new_even[y, rows, :] = full_n


def close_body(plan, flags, table, even_ref, odd_ref, rest_ref, *refs):
    got, field = refs[:-1], refs[-1]
    shape = (plan.half, plan.nx)
    rising_z = column(table, 6, shape) > 0
    get_p, get_n = member_reader(
        plan, flags[0] == 0, (even_ref, odd_ref, rest_ref), got, column(table, 3, shape)
    )
    for y in range(plan.ny):
        for z in range(plan.nz):
            row = y * plan.nz + z
            p = get_p(z, y)
            n = get_n(z, y)
            field[pl.ds(row, plan.half, stride=plan.rows), :] = jnp.where(rising_z, p, n)
            field[pl.ds(row + plan.half * plan.rows, plan.half, stride=plan.rows), :] = jnp.where(
                rising_z, n, p
            )


def call(body, outs, args, scratch=()):
    in_specs = [pl.BlockSpec(memory_space=SMEM)] + [pl.BlockSpec(memory_space=VMEM)] * (len(args) - 1)
    moved = sum(math.prod(a.shape) * 4 for a in list(args) + list(outs))
    return pl.pallas_call(
        body,
        out_shape=outs,
        in_specs=in_specs,
        out_specs=[pl.BlockSpec(memory_space=VMEM)] * len(outs),
        scratch_shapes=list(scratch),
        cost_estimate=pl.CostEstimate(flops=8 * moved, bytes_accessed=moved, transcendentals=0),
        compiler_params=pltpu.CompilerParams(vmem_limit_bytes=32 << 20),
    )(*args)


def shards(fodf, directions, signs):
    plan = Plan(fodf.shape, lax.axis_size("gz"), lax.axis_size("gy"))
    half = plan.half
    flags = jnp.stack([lax.axis_index("gz") % 2, lax.axis_index("gy") % 2]).astype(jnp.int32)
    near = directions[:, :half]
    turn = signs[:, :half].astype(jnp.float32)
    speeds = TIME_STEP * jnp.abs(near)
    columns = jnp.concatenate(
        [1.0 - jnp.sum(speeds, 0, keepdims=True), speeds, turn[:2] * turn[2:], turn[2:]], 0
    )
    table = columns.T
    field = fodf.reshape(plan.field.shape)
    edge_outs = [plan.edge] * (1 + plan.y_two)
    state_outs = [plan.layer, plan.layer, plan.rest]
    opened = call(
        functools.partial(open_body, plan), state_outs + edge_outs, [flags, table, field]
    )
    state, edges = opened[:3], opened[3:]
    matrix = angular_matrix(near)
    got = []
    for step in range(ITERS):
        if step > 0:
            edges = call(
                functools.partial(edge_body, plan), edge_outs, [flags, table, *state, *got]
            )
        arriving = exchange(state[0], state[1], "gz")
        y_got = exchange(edges[0], edges[-1], "gy")
        state = call(
            functools.partial(step_body, plan, step == 0),
            state_outs,
            [flags, table, matrix, *state, *got, *y_got],
            [
                VMEM((2, plan.nz, plan.ny + 2, half, plan.nx), jnp.float32),
                VMEM((half, plan.rows * plan.nx), jnp.float32),
                VMEM((half, plan.rows * plan.nx), jnp.float32),
            ],
        )
        got = arriving
    field = call(
        functools.partial(close_body, plan), [plan.field], [flags, table, *state, *got]
    )[0]
    return field.reshape(fodf.shape)


def solution(mesh):
    placed = (P(None, "gy", "gz", None), P(), P())
    return jax.shard_map(
        shards, mesh=mesh, in_specs=placed, out_specs=P(None, "gy", "gz", None), check_vma=False
    )
```

```python
import functools
import math

import jax
import jax.numpy as jnp
from jax import lax
from jax.experimental import pallas as pl
from jax.experimental.pallas import tpu as pltpu
from jax.sharding import PartitionSpec as P

LMAX = 8
ITERS = 4
TIME_STEP = 0.5
DIFFUSION = 0.02

VMEM = pltpu.VMEM
SMEM = pltpu.SMEM


def double_factorial(value):
    result = 1
    while value > 1:
        result = result * value
        value = value - 2
    return result


def harmonic_rows(directions):
    along_x, along_y, along_z = (directions[0], directions[1], directions[2])
    cosines = [jnp.ones_like(along_x)]
    sines = [jnp.zeros_like(along_x)]
    for order in range(1, LMAX + 1):
        cosines.append(cosines[-1] * along_x - sines[-1] * along_y)
        sines.append(cosines[-2] * along_y + sines[-1] * along_x)
    legendre = {}
    for order in range(LMAX + 1):
        legendre[order, order] = double_factorial(2 * order - 1) * jnp.ones_like(along_z)
        if order + 1 <= LMAX:
            legendre[order + 1, order] = (2 * order + 1) * along_z * legendre[order, order]
        for degree in range(order + 2, LMAX + 1):
            legendre[degree, order] = (
                (2 * degree - 1) * along_z * legendre[degree - 1, order]
                - (degree + order - 1) * legendre[degree - 2, order]
            ) / (degree - order)
    basis_rows = []
    eigen_values = []
    for degree in range(0, LMAX + 1, 2):
        for order in range(degree + 1):
            weight_norm = math.sqrt(
                (2 * degree + 1) * math.factorial(degree - order) / math.factorial(degree + order)
            )
            basis_rows.append(weight_norm * legendre[degree, order] * cosines[order])
            eigen_values.append(-float(degree * (degree + 1)))
            if order > 0:
                basis_rows.append(weight_norm * legendre[degree, order] * sines[order])
                eigen_values.append(-float(degree * (degree + 1)))
    return (jnp.stack(basis_rows, 0), jnp.array(eigen_values, dtype=directions.dtype))


def angular_matrix(half):
    basis, eigen_values = harmonic_rows(half)
    gram = 2.0 * jnp.dot(basis, basis.T, precision=lax.Precision.HIGHEST)
    chol_lower = jnp.linalg.cholesky(gram)
    partial_solve = lax.linalg.triangular_solve(chol_lower, basis, left_side=True, lower=True)
    analysis = lax.linalg.triangular_solve(
        chol_lower, partial_solve, left_side=True, lower=True, transpose_a=True
    )
    synthesis = basis.T * (TIME_STEP * DIFFUSION * eigen_values)[None, :]
    return jnp.dot(synthesis, analysis, precision=lax.Precision.HIGHEST)


def exchange(even_load, odd_load, axis):
    peers = lax.axis_size(axis)
    first = [(i, i ^ 1) for i in range(peers)]
    second = [(i, i + 1 if i % 2 else i - 1) for i in range(1, peers - 1)]
    got = [lax.ppermute(even_load, axis, first)]
    if second:
        got.append(lax.ppermute(odd_load, axis, second))
    return got


class Plan:
    def __init__(self, shape, z_peers, y_peers):
        self.kk, self.ny, self.nz, self.nx = shape
        self.half = self.kk // 2
        self.rows = self.ny * self.nz
        self.z_two = z_peers > 2
        self.y_two = y_peers > 2
        self.layer = jax.ShapeDtypeStruct((self.ny, self.half, self.nx), jnp.float32)
        self.rest = jax.ShapeDtypeStruct((2, self.nz - 1, self.ny, self.half, self.nx), jnp.float32)
        self.edge = jax.ShapeDtypeStruct((self.nz, self.half, self.nx), jnp.float32)
        self.field = jax.ShapeDtypeStruct((self.kk * self.rows, self.nx), jnp.float32)


def column(table, index, shape):
    return jnp.broadcast_to(table[:, index : index + 1], shape)


def from_below(even, got):
    first = got[0]
    if len(got) == 1:
        return jnp.where(even, jnp.zeros_like(first), first)
    return jnp.where(even, got[1], first)


def from_above(even, got):
    first = got[0]
    if len(got) == 1:
        return jnp.where(even, first, jnp.zeros_like(first))
    return jnp.where(even, first, got[1])


def write_edges(even, rising_y, get_p, get_n, plan, outs):
    for z in range(plan.nz):
        top, low = plan.ny - 1, 0
        up = jnp.where(rising_y, get_p(z, top), get_n(z, top))
        down = jnp.where(rising_y, get_n(z, low), get_p(z, low))
        outs[0][z] = jnp.where(even, up, down)
        if plan.y_two:
            outs[1][z] = jnp.where(even, down, up)


def open_body(plan, flags, table, field, even_ref, odd_ref, rest_ref, *edges):
    shape = (plan.half, plan.nx)
    even = flags[0] == 0
    rising_z = column(table, 6, shape) > 0
    rising_y = column(table, 5, shape) > 0
    kept = {}
    for y in range(plan.ny):
        for z in range(plan.nz):
            row = y * plan.nz + z
            a = field[pl.ds(row, plan.half, stride=plan.rows), :]
            b = field[pl.ds(row + plan.half * plan.rows, plan.half, stride=plan.rows), :]
            p = jnp.where(rising_z, a, b)
            n = jnp.where(rising_z, b, a)
            if z < plan.nz - 1:
                rest_ref[0, z, y] = p
            if z > 0:
                rest_ref[1, z - 1, y] = n
            if z == plan.nz - 1:
                top = p
            if z == 0:
                bottom = n
            if y in (0, plan.ny - 1):
                kept[z, y] = (p, n)
        even_ref[y] = jnp.where(even, top, bottom)
        odd_ref[y] = jnp.where(even, bottom, top)
    write_edges(
        flags[1] == 0,
        rising_y,
        lambda z, y: kept[z, y][0],
        lambda z, y: kept[z, y][1],
        plan,
        edges,
    )


def member_reader(plan, even, state, got, speed_z):
    even_ref, odd_ref, rest_ref = state

    def get_p(z, y):
        if z == plan.nz - 1:
            return jnp.where(even, even_ref[y], odd_ref[y])
        value = rest_ref[0, z, y]
        if got is not None and z == 0:
            value = value + speed_z * from_below(even, [g[y] for g in got])
        return value

    def get_n(z, y):
        if z == 0:
            return jnp.where(even, odd_ref[y], even_ref[y])
        value = rest_ref[1, z - 1, y]
        if got is not None and z == plan.nz - 1:
            value = value + speed_z * from_above(even, [g[y] for g in got])
        return value

    return get_p, get_n


def edge_body(plan, flags, table, even_ref, odd_ref, rest_ref, *refs):
    count = 1 + plan.z_two
    got, edges = refs[:count], refs[count:]
    shape = (plan.half, plan.nx)
    get_p, get_n = member_reader(
        plan, flags[0] == 0, (even_ref, odd_ref, rest_ref), got, column(table, 3, shape)
    )
    write_edges(flags[1] == 0, column(table, 5, shape) > 0, get_p, get_n, plan, edges)


def split(value):
    high = value.astype(jnp.bfloat16)
    low = (value - high.astype(jnp.float32)).astype(jnp.bfloat16)
    return high, low


def step_body(plan, first, flags, table, matrix, even_ref, odd_ref, rest_ref, *refs):
    z_count = 0 if first else 1 + plan.z_two
    y_count = 1 + plan.y_two
    got = None if first else refs[:z_count]
    y_got = refs[z_count : z_count + y_count]
    new_even, new_odd, new_rest, full, highs, lows, turn = refs[z_count + y_count :]
    half, nx, ny, nz = plan.half, plan.nx, plan.ny, plan.nz
    even = flags[0] == 0
    y_even = flags[1] == 0
    for part in range(half // 16):
        rows = pl.ds(part * 16, 16)
        speed_z = column(table[rows, :], 3, (16, nx))
        for z in range(nz):
            low = from_below(y_even, [g[z, rows, :] for g in y_got])
            high = from_above(y_even, [g[z, rows, :] for g in y_got])
            full[0, z, 0, rows, :] = low
            full[1, z, 0, rows, :] = low
            full[0, z, ny + 1, rows, :] = high
            full[1, z, ny + 1, rows, :] = high
        for y in range(ny):
            for z in range(nz):
                if z == nz - 1:
                    p = jnp.where(even, even_ref[y, rows, :], odd_ref[y, rows, :])
                else:
                    p = rest_ref[0, z, y, rows, :]
                    if got is not None and z == 0:
                        p = p + speed_z * from_below(even, [g[y, rows, :] for g in got])
                if z == 0:
                    n = jnp.where(even, odd_ref[y, rows, :], even_ref[y, rows, :])
                else:
                    n = rest_ref[1, z - 1, y, rows, :]
                    if got is not None and z == nz - 1:
                        n = n + speed_z * from_above(even, [g[y, rows, :] for g in got])
                full[0, z, y + 1, rows, :] = p
                full[1, z, y + 1, rows, :] = n
                row = y * nz + z
                high, low = split(p + n)
                highs[rows, row * nx : (row + 1) * nx] = high
                lows[rows, row * nx : (row + 1) * nx] = low
    m_high, m_low = split(matrix[...])
    width = nz * nx
    for y in range(ny):
        cols = slice(y * width, (y + 1) * width)
        high = highs[:, cols]
        turn[:, cols] = (
            jnp.dot(m_high, high, preferred_element_type=jnp.float32)
            + jnp.dot(m_low, high, preferred_element_type=jnp.float32)
            + jnp.dot(m_high, lows[:, cols], preferred_element_type=jnp.float32)
        )
    tile = (8, nx)
    lane = lax.broadcasted_iota(jnp.int32, tile, 1)
    first_lane = lane == 0
    last_lane = lane == nx - 1
    for part in range(half // 8):
        rows = pl.ds(part * 8, 8)
        tab = table[rows, :]
        rest_speed = column(tab, 0, tile)
        speed_x = column(tab, 1, tile)
        speed_y = column(tab, 2, tile)
        speed_z = column(tab, 3, tile)
        rising_x = column(tab, 4, tile) > 0
        rising_y = column(tab, 5, tile) > 0
        for y in range(ny):
            ps = [full[0, z, y + 1, rows, :] for z in range(nz)]
            ns = [full[1, z, y + 1, rows, :] for z in range(nz)]
            for z in range(nz):
                row = y * nz + z
                p, n = ps[z], ns[z]
                u = jnp.where(rising_x, p, n)
                v = jnp.where(rising_x, n, p)
                u = jnp.where(first_lane, 0.0, pltpu.roll(u, 1, 1))
                v = jnp.where(last_lane, 0.0, pltpu.roll(v, nx - 1, 1))
                angular = turn[rows, row * nx : (row + 1) * nx]
                new_p = rest_speed * p + speed_x * jnp.where(rising_x, u, v) + angular
                new_n = rest_speed * n + speed_x * jnp.where(rising_x, v, u) + angular
                new_p = new_p + speed_y * jnp.where(
                    rising_y, full[0, z, y, rows, :], full[0, z, y + 2, rows, :]
                )
                new_n = new_n + speed_y * jnp.where(
                    rising_y, full[1, z, y + 2, rows, :], full[1, z, y, rows, :]
                )
                if z > 0:
                    new_p = new_p + speed_z * ps[z - 1]
                if z < nz - 1:
                    new_n = new_n + speed_z * ns[z + 1]
                if z < nz - 1:
                    new_rest[0, z, y, rows, :] = new_p
                else:
                    top = new_p
                if z > 0:
                    new_rest[1, z - 1, y, rows, :] = new_n
                else:
                    bottom = new_n
            new_even[y, rows, :] = jnp.where(even, top, bottom)
            new_odd[y, rows, :] = jnp.where(even, bottom, top)


def close_body(plan, flags, table, even_ref, odd_ref, rest_ref, *refs):
    got, field = refs[:-1], refs[-1]
    shape = (plan.half, plan.nx)
    rising_z = column(table, 6, shape) > 0
    get_p, get_n = member_reader(
        plan, flags[0] == 0, (even_ref, odd_ref, rest_ref), got, column(table, 3, shape)
    )
    for y in range(plan.ny):
        for z in range(plan.nz):
            row = y * plan.nz + z
            p = get_p(z, y)
            n = get_n(z, y)
            field[pl.ds(row, plan.half, stride=plan.rows), :] = jnp.where(rising_z, p, n)
            field[pl.ds(row + plan.half * plan.rows, plan.half, stride=plan.rows), :] = jnp.where(
                rising_z, n, p
            )


def call(body, outs, args, scratch=()):
    in_specs = [pl.BlockSpec(memory_space=SMEM)] + [pl.BlockSpec(memory_space=VMEM)] * (len(args) - 1)
    moved = sum(math.prod(a.shape) * 4 for a in list(args) + list(outs))
    return pl.pallas_call(
        body,
        out_shape=outs,
        in_specs=in_specs,
        out_specs=[pl.BlockSpec(memory_space=VMEM)] * len(outs),
        scratch_shapes=list(scratch),
        cost_estimate=pl.CostEstimate(flops=8 * moved, bytes_accessed=moved, transcendentals=0),
        compiler_params=pltpu.CompilerParams(vmem_limit_bytes=32 << 20),
    )(*args)


def shards(fodf, directions, signs):
    plan = Plan(fodf.shape, lax.axis_size("gz"), lax.axis_size("gy"))
    half = plan.half
    flags = jnp.stack([lax.axis_index("gz") % 2, lax.axis_index("gy") % 2]).astype(jnp.int32)
    near = directions[:, :half]
    turn = signs[:, :half].astype(jnp.float32)
    speeds = TIME_STEP * jnp.abs(near)
    columns = jnp.concatenate(
        [1.0 - jnp.sum(speeds, 0, keepdims=True), speeds, turn[:2] * turn[2:], turn[2:]], 0
    )
    table = columns.T
    field = fodf.reshape(plan.field.shape)
    edge_outs = [plan.edge] * (1 + plan.y_two)
    state_outs = [plan.layer, plan.layer, plan.rest]
    opened = call(
        functools.partial(open_body, plan), state_outs + edge_outs, [flags, table, field]
    )
    state, edges = opened[:3], opened[3:]
    matrix = angular_matrix(near)
    got = []
    for step in range(ITERS):
        if step > 0:
            edges = call(
                functools.partial(edge_body, plan), edge_outs, [flags, table, *state, *got]
            )
        arriving = exchange(state[0], state[1], "gz")
        y_got = exchange(edges[0], edges[-1], "gy")
        state = call(
            functools.partial(step_body, plan, step == 0),
            state_outs,
            [flags, table, matrix, *state, *got, *y_got],
            [
                VMEM((2, plan.nz, plan.ny + 2, half, plan.nx), jnp.float32),
                VMEM((half, plan.rows * plan.nx), jnp.bfloat16),
                VMEM((half, plan.rows * plan.nx), jnp.bfloat16),
                VMEM((half, plan.rows * plan.nx), jnp.float32),
            ],
        )
        got = arriving
    field = call(
        functools.partial(close_body, plan), [plan.field], [flags, table, *state, *got]
    )[0]
    return field.reshape(fodf.shape)


def solution(mesh):
    placed = (P(None, "gy", "gz", None), P(), P())
    return jax.shard_map(
        shards, mesh=mesh, in_specs=placed, out_specs=P(None, "gy", "gz", None), check_vma=False
    )
```

```python
import functools
import math

import jax
import jax.numpy as jnp
from jax import lax
from jax.experimental import pallas as pl
from jax.experimental.pallas import tpu as pltpu
from jax.sharding import PartitionSpec as P


LMAX = 8
ITERS = 4
TIME_STEP = 0.5
DIFFUSION = 0.02

VMEM = pltpu.VMEM


def double_factorial(value):
    result = 1
    while value > 1:
        result = result * value
        value = value - 2
    return result


def harmonic_rows(directions):
    along_x, along_y, along_z = (directions[0], directions[1], directions[2])
    cosines = [jnp.ones_like(along_x)]
    sines = [jnp.zeros_like(along_x)]
    for _ in range(1, LMAX + 1):
        cosines.append(cosines[-1] * along_x - sines[-1] * along_y)
        sines.append(cosines[-2] * along_y + sines[-1] * along_x)
    legendre = {}
    for order in range(LMAX + 1):
        legendre[order, order] = double_factorial(2 * order - 1) * jnp.ones_like(along_z)
        if order + 1 <= LMAX:
            legendre[order + 1, order] = (2 * order + 1) * along_z * legendre[order, order]
        for degree in range(order + 2, LMAX + 1):
            legendre[degree, order] = (
                (2 * degree - 1) * along_z * legendre[degree - 1, order]
                - (degree + order - 1) * legendre[degree - 2, order]
            ) / (degree - order)
    basis_rows = []
    eigen_values = []
    for degree in range(0, LMAX + 1, 2):
        for order in range(degree + 1):
            weight_norm = math.sqrt(
                (2 * degree + 1) * math.factorial(degree - order) / math.factorial(degree + order)
            )
            basis_rows.append(weight_norm * legendre[degree, order] * cosines[order])
            eigen_values.append(-float(degree * (degree + 1)))
            if order > 0:
                basis_rows.append(weight_norm * legendre[degree, order] * sines[order])
                eigen_values.append(-float(degree * (degree + 1)))
    return (jnp.stack(basis_rows, 0), jnp.array(eigen_values, dtype=directions.dtype))


def angular_matrix(half):
    basis, eigen_values = harmonic_rows(half)
    gram = 2.0 * jnp.dot(basis, basis.T, precision=lax.Precision.HIGHEST)
    chol_lower = jnp.linalg.cholesky(gram)
    partial_solve = lax.linalg.triangular_solve(chol_lower, basis, left_side=True, lower=True)
    analysis = lax.linalg.triangular_solve(
        chol_lower, partial_solve, left_side=True, lower=True, transpose_a=True
    )
    synthesis = basis.T * (TIME_STEP * DIFFUSION * eigen_values)[None, :]
    return jnp.dot(synthesis, analysis, precision=lax.Precision.HIGHEST)


def exchange(even_load, odd_load, axis):
    peers = lax.axis_size(axis)
    first = [(i, i ^ 1) for i in range(peers)]
    second = [(i, i + 1 if i % 2 else i - 1) for i in range(1, peers - 1)]
    got = [lax.ppermute(even_load, axis, first)]
    if second:
        got.append(lax.ppermute(odd_load, axis, second))
    return got


class Plan:
    def __init__(self, shape, z_peers, y_peers):
        self.kk, self.ny, self.nz, self.nx = shape
        self.half = self.kk // 2
        self.rows = self.ny * self.nz
        self.chunks = 3
        self.z_two = z_peers > 2
        self.y_two = y_peers > 2
        self.layer = jax.ShapeDtypeStruct((self.ny, self.half, self.nx), jnp.float32)
        self.rest = jax.ShapeDtypeStruct((2, self.nz - 1, self.ny, self.half, self.nx), jnp.float32)
        self.edge = jax.ShapeDtypeStruct((self.nz, self.half, self.nx), jnp.float32)
        self.field = jax.ShapeDtypeStruct((self.kk * self.rows, self.nx), jnp.float32)


def is_even(axis):
    return lax.rem(lax.axis_index(axis), 2) == 0


def column(table, index, shape):
    return jnp.broadcast_to(table[:, index : index + 1], shape)


def from_below(even, got):
    first = got[0]
    if len(got) == 1:
        return jnp.where(even, jnp.zeros_like(first), first)
    return jnp.where(even, got[1], first)


def from_above(even, got):
    first = got[0]
    if len(got) == 1:
        return jnp.where(even, first, jnp.zeros_like(first))
    return jnp.where(even, first, got[1])


def write_edges(even, rising_y, get_p, get_n, plan, outs):
    for z in range(plan.nz):
        top, low = plan.ny - 1, 0
        up = jnp.where(rising_y, get_p(z, top), get_n(z, top))
        down = jnp.where(rising_y, get_n(z, low), get_p(z, low))
        outs[0][z] = jnp.where(even, up, down)
        if plan.y_two:
            outs[1][z] = jnp.where(even, down, up)


def row_to_column(row, size):
    square = jnp.broadcast_to(row, (size, size))
    same = lax.broadcasted_iota(jnp.int32, (size, size), 0) == lax.broadcasted_iota(
        jnp.int32, (size, size), 1
    )
    return jnp.sum(jnp.where(same, square, 0.0), axis=1, keepdims=True)


def field_copies(plan, source, target, sems):
    copies = []
    depth = plan.half // plan.chunks * plan.rows
    for chunk in range(plan.chunks):
        for member in range(2):
            where = pl.ds((member * plan.chunks + chunk) * depth, depth)
            copies.append(
                pltpu.make_async_copy(source.at[where], target.at[where], sems.at[chunk, member])
            )
    return copies


def load_pair(plan, held, start, size, row):
    pair = []
    for member in range(2):
        base = (member * plan.half + start) * plan.rows + row
        pair.append(held[pl.ds(base, size, stride=plan.rows), :])
    return pair


def send_body(plan, signs_raw, field_raw, even_ref, odd_ref, signs, field, sems, small):
    fetch = pltpu.make_async_copy(signs_raw, signs, small)
    fetch.start()
    copies = field_copies(plan, field_raw, field, sems)
    for copy in copies:
        copy.start()
    fetch.wait()
    even = is_even("gz")
    signs_z = signs[2:3, : plan.half].astype(jnp.float32)
    turn = jnp.broadcast_to(row_to_column(signs_z, plan.half), (plan.half, plan.nx))
    size = plan.half // plan.chunks
    for chunk in range(plan.chunks):
        copies[2 * chunk].wait()
        copies[2 * chunk + 1].wait()
        start = chunk * size
        rising_z = turn[start : start + size] > 0
        rows = pl.ds(start, size)
        for y in range(plan.ny):
            a, b = load_pair(plan, field, start, size, y * plan.nz + plan.nz - 1)
            top = jnp.where(rising_z, a, b)
            a, b = load_pair(plan, field, start, size, y * plan.nz)
            bottom = jnp.where(rising_z, b, a)
            even_ref[y, rows, :] = jnp.where(even, top, bottom)
            odd_ref[y, rows, :] = jnp.where(even, bottom, top)


def open_body(plan, table, field_raw, rest_ref, *refs):
    edges, (field, sems) = refs[:-2], refs[-2:]
    copies = field_copies(plan, field_raw, field, sems)
    for copy in copies:
        copy.start()
    for copy in copies:
        copy.wait()
    shape = (plan.half, plan.nx)
    rising_z = column(table, 6, shape) > 0
    rising_y = column(table, 5, shape) > 0
    kept = {}
    for y in range(plan.ny):
        for z in range(plan.nz):
            a, b = load_pair(plan, field, 0, plan.half, y * plan.nz + z)
            p = jnp.where(rising_z, a, b)
            n = jnp.where(rising_z, b, a)
            if z < plan.nz - 1:
                rest_ref[0, z, y] = p
            if z > 0:
                rest_ref[1, z - 1, y] = n
            if y in (0, plan.ny - 1):
                kept[z, y] = (p, n)
    write_edges(
        is_even("gy"),
        rising_y,
        lambda z, y: kept[z, y][0],
        lambda z, y: kept[z, y][1],
        plan,
        edges,
    )


def member_reader(plan, even, state, got, speed_z):
    even_ref, odd_ref, rest_ref = state

    def get_p(z, y):
        if z == plan.nz - 1:
            return jnp.where(even, even_ref[y], odd_ref[y])
        value = rest_ref[0, z, y]
        if got is not None and z == 0:
            value = value + speed_z * from_below(even, [g[y] for g in got])
        return value

    def get_n(z, y):
        if z == 0:
            return jnp.where(even, odd_ref[y], even_ref[y])
        value = rest_ref[1, z - 1, y]
        if got is not None and z == plan.nz - 1:
            value = value + speed_z * from_above(even, [g[y] for g in got])
        return value

    return get_p, get_n


def edge_body(plan, table, even_ref, odd_ref, rest_ref, *refs):
    count = 1 + plan.z_two
    got, edges = refs[:count], refs[count:]
    shape = (plan.half, plan.nx)
    get_p, get_n = member_reader(
        plan, is_even("gz"), (even_ref, odd_ref, rest_ref), got, column(table, 3, shape)
    )
    write_edges(is_even("gy"), column(table, 5, shape) > 0, get_p, get_n, plan, edges)


def split(value):
    high = value.astype(jnp.bfloat16)
    low = (value - high.astype(jnp.float32)).astype(jnp.bfloat16)
    return high, low


def step_body(plan, first, table, matrix, even_ref, odd_ref, rest_ref, *refs):
    z_count = 0 if first else 1 + plan.z_two
    y_count = 1 + plan.y_two
    got = None if first else refs[:z_count]
    y_got = refs[z_count : z_count + y_count]
    new_even, new_odd, new_rest, full, highs, lows, turn = refs[z_count + y_count :]
    half, nx, ny, nz = plan.half, plan.nx, plan.ny, plan.nz
    even = is_even("gz")
    y_even = is_even("gy")
    for part in range(half // 16):
        rows = pl.ds(part * 16, 16)
        speed_z = column(table[rows, :], 3, (16, nx))
        for z in range(nz):
            low = from_below(y_even, [g[z, rows, :] for g in y_got])
            high = from_above(y_even, [g[z, rows, :] for g in y_got])
            full[0, z, 0, rows, :] = low
            full[1, z, 0, rows, :] = low
            full[0, z, ny + 1, rows, :] = high
            full[1, z, ny + 1, rows, :] = high
        for y in range(ny):
            for z in range(nz):
                if z == nz - 1:
                    p = jnp.where(even, even_ref[y, rows, :], odd_ref[y, rows, :])
                else:
                    p = rest_ref[0, z, y, rows, :]
                    if got is not None and z == 0:
                        p = p + speed_z * from_below(even, [g[y, rows, :] for g in got])
                if z == 0:
                    n = jnp.where(even, odd_ref[y, rows, :], even_ref[y, rows, :])
                else:
                    n = rest_ref[1, z - 1, y, rows, :]
                    if got is not None and z == nz - 1:
                        n = n + speed_z * from_above(even, [g[y, rows, :] for g in got])
                full[0, z, y + 1, rows, :] = p
                full[1, z, y + 1, rows, :] = n
                row = y * nz + z
                high, low = split(p + n)
                highs[rows, row * nx : (row + 1) * nx] = high
                lows[rows, row * nx : (row + 1) * nx] = low
    m_high, m_low = split(matrix[...])
    width = nz * nx
    for y in range(ny):
        cols = slice(y * width, (y + 1) * width)
        high = highs[:, cols]
        turn[:, cols] = (
            jnp.dot(m_high, high, preferred_element_type=jnp.float32)
            + jnp.dot(m_low, high, preferred_element_type=jnp.float32)
            + jnp.dot(m_high, lows[:, cols], preferred_element_type=jnp.float32)
        )
    tile = (8, nx)
    lane = lax.broadcasted_iota(jnp.int32, tile, 1)
    first_lane = lane == 0
    last_lane = lane == nx - 1
    for part in range(half // 8):
        rows = pl.ds(part * 8, 8)
        tab = table[rows, :]
        rest_speed = column(tab, 0, tile)
        speed_x = column(tab, 1, tile)
        speed_y = column(tab, 2, tile)
        speed_z = column(tab, 3, tile)
        rising_x = column(tab, 4, tile) > 0
        rising_y = column(tab, 5, tile) > 0
        for y in range(ny):
            ps = [full[0, z, y + 1, rows, :] for z in range(nz)]
            ns = [full[1, z, y + 1, rows, :] for z in range(nz)]
            for z in range(nz):
                row = y * nz + z
                p, n = ps[z], ns[z]
                u = jnp.where(rising_x, p, n)
                v = jnp.where(rising_x, n, p)
                u = jnp.where(first_lane, 0.0, pltpu.roll(u, 1, 1))
                v = jnp.where(last_lane, 0.0, pltpu.roll(v, nx - 1, 1))
                angular = turn[rows, row * nx : (row + 1) * nx]
                new_p = rest_speed * p + speed_x * jnp.where(rising_x, u, v) + angular
                new_n = rest_speed * n + speed_x * jnp.where(rising_x, v, u) + angular
                new_p = new_p + speed_y * jnp.where(
                    rising_y, full[0, z, y, rows, :], full[0, z, y + 2, rows, :]
                )
                new_n = new_n + speed_y * jnp.where(
                    rising_y, full[1, z, y + 2, rows, :], full[1, z, y, rows, :]
                )
                if z > 0:
                    new_p = new_p + speed_z * ps[z - 1]
                if z < nz - 1:
                    new_n = new_n + speed_z * ns[z + 1]
                if z < nz - 1:
                    new_rest[0, z, y, rows, :] = new_p
                else:
                    top = new_p
                if z > 0:
                    new_rest[1, z - 1, y, rows, :] = new_n
                else:
                    bottom = new_n
            new_even[y, rows, :] = jnp.where(even, top, bottom)
            new_odd[y, rows, :] = jnp.where(even, bottom, top)


def close_body(plan, table, even_ref, odd_ref, rest_ref, *refs):
    got, (field, held, sems) = refs[:-3], refs[-3:]
    copies = field_copies(plan, held, field, sems)
    even = is_even("gz")
    nz = plan.nz
    size = plan.half // plan.chunks
    for chunk in range(plan.chunks):
        start = chunk * size
        rows = pl.ds(start, size)
        tab = table[rows, :]
        rising_z = column(tab, 6, (size, plan.nx)) > 0
        speed_z = column(tab, 3, (size, plan.nx))
        for y in range(plan.ny):
            arrived = [g[y, rows, :] for g in got]
            low = speed_z * from_below(even, arrived)
            high = speed_z * from_above(even, arrived)
            one, two = even_ref[y, rows, :], odd_ref[y, rows, :]
            for z in range(nz):
                if z == nz - 1:
                    p = jnp.where(even, one, two)
                else:
                    p = rest_ref[0, z, y, rows, :]
                if z == 0:
                    n = jnp.where(even, two, one)
                else:
                    n = rest_ref[1, z - 1, y, rows, :]
                if z == 0:
                    p = p + low
                if z == nz - 1:
                    n = n + high
                base = start * plan.rows + y * nz + z
                held[pl.ds(base, size, stride=plan.rows), :] = jnp.where(rising_z, p, n)
                base = base + plan.half * plan.rows
                held[pl.ds(base, size, stride=plan.rows), :] = jnp.where(rising_z, n, p)
        copies[2 * chunk].start()
        copies[2 * chunk + 1].start()
    for copy in copies:
        copy.wait()


def stay(value):
    return pltpu.with_memory_space_constraint(value, pltpu.HBM)


def call(body, outs, args, scratch=(), raw_in=(), raw_out=False):
    in_specs = []
    for i in range(len(args)):
        in_specs.append(pl.BlockSpec(memory_space=pltpu.HBM if i in raw_in else VMEM))
    moved = sum(math.prod(a.shape) * 4 for a in list(args) + list(outs))
    return pl.pallas_call(
        body,
        out_shape=outs,
        in_specs=in_specs,
        out_specs=[pl.BlockSpec(memory_space=pltpu.HBM if raw_out else VMEM)] * len(outs),
        scratch_shapes=list(scratch),
        cost_estimate=pl.CostEstimate(flops=8 * moved, bytes_accessed=moved, transcendentals=0),
        compiler_params=pltpu.CompilerParams(vmem_limit_bytes=32 << 20),
    )(*args)


def shards(fodf, directions, signs):
    plan = Plan(fodf.shape, lax.axis_size("gz"), lax.axis_size("gy"))
    half = plan.half
    field = fodf.reshape(plan.field.shape)
    edge_outs = [plan.edge] * (1 + plan.y_two)
    state_outs = [plan.layer, plan.layer, plan.rest]
    streamed = [
        VMEM(plan.field.shape, jnp.float32),
        pltpu.SemaphoreType.DMA((plan.chunks, 2)),
    ]
    first, second = call(
        functools.partial(send_body, plan),
        [plan.layer, plan.layer],
        [stay(signs), stay(field)],
        [VMEM(signs.shape, signs.dtype), *streamed, pltpu.SemaphoreType.DMA],
        raw_in=(0, 1),
    )
    later, signs, directions, first, second = lax.optimization_barrier(
        (field, signs, directions, first, second)
    )
    near = directions[:, :half]
    turn = signs[:, :half].astype(jnp.float32)
    speeds = TIME_STEP * jnp.abs(near)
    columns = jnp.concatenate(
        [1.0 - jnp.sum(speeds, 0, keepdims=True), speeds, turn[:2] * turn[2:], turn[2:]], 0
    )
    table = columns.T
    opened = call(
        functools.partial(open_body, plan),
        [plan.rest] + edge_outs,
        [table, stay(later)],
        streamed,
        raw_in=(1,),
    )
    state, edges = [first, second, opened[0]], opened[1:]
    matrix = angular_matrix(near)
    got = []
    for step in range(ITERS):
        if step > 0:
            edges = call(
                functools.partial(edge_body, plan), edge_outs, [table, *state, *got]
            )
        arriving = exchange(state[0], state[1], "gz")
        y_got = exchange(edges[0], edges[-1], "gy")
        state = call(
            functools.partial(step_body, plan, step == 0),
            state_outs,
            [table, matrix, *state, *got, *y_got],
            [
                VMEM((2, plan.nz, plan.ny + 2, half, plan.nx), jnp.float32),
                VMEM((half, plan.rows * plan.nx), jnp.bfloat16),
                VMEM((half, plan.rows * plan.nx), jnp.bfloat16),
                VMEM((half, plan.rows * plan.nx), jnp.float32),
            ],
        )
        got = arriving
    field = call(
        functools.partial(close_body, plan),
        [plan.field],
        [table, *state, *got],
        streamed,
        raw_out=True,
    )[0]
    return field.reshape(fodf.shape)


def solution(mesh):
    placed = (P(None, "gy", "gz", None), P(), P())
    return jax.shard_map(
        shards, mesh=mesh, in_specs=placed, out_specs=P(None, "gy", "gz", None), check_vma=False
    )
```

```python
import functools
import math

import jax
import jax.numpy as jnp
from jax import lax
from jax.experimental import pallas as pl
from jax.experimental.pallas import tpu as pltpu
from jax.sharding import PartitionSpec as P


LMAX = 8
ITERS = 4
TIME_STEP = 0.5
DIFFUSION = 0.02

VMEM = pltpu.VMEM


def double_factorial(value):
    result = 1
    while value > 1:
        result = result * value
        value = value - 2
    return result


def harmonic_rows(directions):
    along_x, along_y, along_z = (directions[0], directions[1], directions[2])
    cosines = [jnp.ones_like(along_x)]
    sines = [jnp.zeros_like(along_x)]
    for _ in range(1, LMAX + 1):
        cosines.append(cosines[-1] * along_x - sines[-1] * along_y)
        sines.append(cosines[-2] * along_y + sines[-1] * along_x)
    legendre = {}
    for order in range(LMAX + 1):
        legendre[order, order] = double_factorial(2 * order - 1) * jnp.ones_like(along_z)
        if order + 1 <= LMAX:
            legendre[order + 1, order] = (2 * order + 1) * along_z * legendre[order, order]
        for degree in range(order + 2, LMAX + 1):
            legendre[degree, order] = (
                (2 * degree - 1) * along_z * legendre[degree - 1, order]
                - (degree + order - 1) * legendre[degree - 2, order]
            ) / (degree - order)
    basis_rows = []
    eigen_values = []
    for degree in range(0, LMAX + 1, 2):
        for order in range(degree + 1):
            weight_norm = math.sqrt(
                (2 * degree + 1) * math.factorial(degree - order) / math.factorial(degree + order)
            )
            basis_rows.append(weight_norm * legendre[degree, order] * cosines[order])
            eigen_values.append(-float(degree * (degree + 1)))
            if order > 0:
                basis_rows.append(weight_norm * legendre[degree, order] * sines[order])
                eigen_values.append(-float(degree * (degree + 1)))
    return (jnp.stack(basis_rows, 0), jnp.array(eigen_values, dtype=directions.dtype))


def angular_matrix(half):
    basis, eigen_values = harmonic_rows(half)
    gram = 2.0 * jnp.dot(basis, basis.T, precision=lax.Precision.HIGHEST)
    chol_lower = jnp.linalg.cholesky(gram)
    partial_solve = lax.linalg.triangular_solve(chol_lower, basis, left_side=True, lower=True)
    analysis = lax.linalg.triangular_solve(
        chol_lower, partial_solve, left_side=True, lower=True, transpose_a=True
    )
    synthesis = basis.T * (TIME_STEP * DIFFUSION * eigen_values)[None, :]
    return jnp.dot(synthesis, analysis, precision=lax.Precision.HIGHEST)


def exchange(even_load, odd_load, axis):
    peers = lax.axis_size(axis)
    first = [(i, i ^ 1) for i in range(peers)]
    second = [(i, i + 1 if i % 2 else i - 1) for i in range(1, peers - 1)]
    got = [lax.ppermute(even_load, axis, first)]
    if second:
        got.append(lax.ppermute(odd_load, axis, second))
    return got


class Plan:
    def __init__(self, shape, z_peers, y_peers):
        self.kk, self.ny, self.nz, self.nx = shape
        self.half = self.kk // 2
        self.rows = self.ny * self.nz
        self.chunks = 3
        self.z_two = z_peers > 2
        self.y_two = y_peers > 2
        self.layer = jax.ShapeDtypeStruct((self.ny, self.half, self.nx), jnp.float32)
        self.rest = jax.ShapeDtypeStruct((2, self.nz - 1, self.ny, self.half, self.nx), jnp.float32)
        self.edge = jax.ShapeDtypeStruct((self.nz, self.half, self.nx), jnp.float32)
        self.field = jax.ShapeDtypeStruct((self.kk * self.rows, self.nx), jnp.float32)


def is_even(axis):
    return lax.rem(lax.axis_index(axis), 2) == 0


def column(table, index, shape):
    return jnp.broadcast_to(table[:, index : index + 1], shape)


def from_below(even, got):
    first = got[0]
    if len(got) == 1:
        return jnp.where(even, jnp.zeros_like(first), first)
    return jnp.where(even, got[1], first)


def from_above(even, got):
    first = got[0]
    if len(got) == 1:
        return jnp.where(even, first, jnp.zeros_like(first))
    return jnp.where(even, first, got[1])


def write_edges(even, rising_y, get_p, get_n, plan, outs):
    for z in range(plan.nz):
        top, low = plan.ny - 1, 0
        up = jnp.where(rising_y, get_p(z, top), get_n(z, top))
        down = jnp.where(rising_y, get_n(z, low), get_p(z, low))
        outs[0][z] = jnp.where(even, up, down)
        if plan.y_two:
            outs[1][z] = jnp.where(even, down, up)


def row_to_column(row, size):
    square = jnp.broadcast_to(row, (size, size))
    same = lax.broadcasted_iota(jnp.int32, (size, size), 0) == lax.broadcasted_iota(
        jnp.int32, (size, size), 1
    )
    return jnp.sum(jnp.where(same, square, 0.0), axis=1, keepdims=True)


def field_copies(plan, source, target, sems):
    copies = []
    depth = plan.half // plan.chunks * plan.rows
    for chunk in range(plan.chunks):
        for member in range(2):
            where = pl.ds((member * plan.chunks + chunk) * depth, depth)
            copies.append(
                pltpu.make_async_copy(source.at[where], target.at[where], sems.at[chunk, member])
            )
    return copies


def load_pair(plan, held, start, size, row):
    pair = []
    for member in range(2):
        base = (member * plan.half + start) * plan.rows + row
        pair.append(held[pl.ds(base, size, stride=plan.rows), :])
    return pair


def send_body(plan, signs_raw, field_raw, even_ref, odd_ref, rest_ref, signs, field, sems, small):
    fetch = pltpu.make_async_copy(signs_raw, signs, small)
    fetch.start()
    copies = field_copies(plan, field_raw, field, sems)
    for copy in copies:
        copy.start()
    fetch.wait()
    even = is_even("gz")
    signs_z = signs[2:3, : plan.half].astype(jnp.float32)
    turn = jnp.broadcast_to(row_to_column(signs_z, plan.half), (plan.half, plan.nx))
    size = plan.half // plan.chunks
    for chunk in range(plan.chunks):
        copies[2 * chunk].wait()
        copies[2 * chunk + 1].wait()
        start = chunk * size
        rising_z = turn[start : start + size] > 0
        rows = pl.ds(start, size)
        for y in range(plan.ny):
            for z in range(plan.nz):
                a, b = load_pair(plan, field, start, size, y * plan.nz + z)
                p = jnp.where(rising_z, a, b)
                n = jnp.where(rising_z, b, a)
                if z < plan.nz - 1:
                    rest_ref[0, z, y, rows, :] = p
                else:
                    top = p
                if z > 0:
                    rest_ref[1, z - 1, y, rows, :] = n
                else:
                    bottom = n
            even_ref[y, rows, :] = jnp.where(even, top, bottom)
            odd_ref[y, rows, :] = jnp.where(even, bottom, top)


def member_reader(plan, even, state, got, speed_z):
    even_ref, odd_ref, rest_ref = state

    def get_p(z, y):
        if z == plan.nz - 1:
            return jnp.where(even, even_ref[y], odd_ref[y])
        value = rest_ref[0, z, y]
        if got is not None and z == 0:
            value = value + speed_z * from_below(even, [g[y] for g in got])
        return value

    def get_n(z, y):
        if z == 0:
            return jnp.where(even, odd_ref[y], even_ref[y])
        value = rest_ref[1, z - 1, y]
        if got is not None and z == plan.nz - 1:
            value = value + speed_z * from_above(even, [g[y] for g in got])
        return value

    return get_p, get_n


def edge_body(plan, first, table, even_ref, odd_ref, rest_ref, *refs):
    count = 0 if first else 1 + plan.z_two
    got, edges = refs[:count] or None, refs[count:]
    shape = (plan.half, plan.nx)
    get_p, get_n = member_reader(
        plan, is_even("gz"), (even_ref, odd_ref, rest_ref), got, column(table, 3, shape)
    )
    write_edges(is_even("gy"), column(table, 5, shape) > 0, get_p, get_n, plan, edges)


def split(value):
    high = value.astype(jnp.bfloat16)
    low = (value - high.astype(jnp.float32)).astype(jnp.bfloat16)
    return high, low


def step_body(plan, first, table, matrix, even_ref, odd_ref, rest_ref, *refs):
    z_count = 0 if first else 1 + plan.z_two
    y_count = 1 + plan.y_two
    got = None if first else refs[:z_count]
    y_got = refs[z_count : z_count + y_count]
    new_even, new_odd, new_rest, full, highs, lows, turn = refs[z_count + y_count :]
    half, nx, ny, nz = plan.half, plan.nx, plan.ny, plan.nz
    even = is_even("gz")
    y_even = is_even("gy")
    for part in range(half // 16):
        rows = pl.ds(part * 16, 16)
        speed_z = column(table[rows, :], 3, (16, nx))
        for z in range(nz):
            low = from_below(y_even, [g[z, rows, :] for g in y_got])
            high = from_above(y_even, [g[z, rows, :] for g in y_got])
            full[0, z, 0, rows, :] = low
            full[1, z, 0, rows, :] = low
            full[0, z, ny + 1, rows, :] = high
            full[1, z, ny + 1, rows, :] = high
        for y in range(ny):
            for z in range(nz):
                if z == nz - 1:
                    p = jnp.where(even, even_ref[y, rows, :], odd_ref[y, rows, :])
                else:
                    p = rest_ref[0, z, y, rows, :]
                    if got is not None and z == 0:
                        p = p + speed_z * from_below(even, [g[y, rows, :] for g in got])
                if z == 0:
                    n = jnp.where(even, odd_ref[y, rows, :], even_ref[y, rows, :])
                else:
                    n = rest_ref[1, z - 1, y, rows, :]
                    if got is not None and z == nz - 1:
                        n = n + speed_z * from_above(even, [g[y, rows, :] for g in got])
                full[0, z, y + 1, rows, :] = p
                full[1, z, y + 1, rows, :] = n
                row = y * nz + z
                high, low = split(p + n)
                highs[rows, row * nx : (row + 1) * nx] = high
                lows[rows, row * nx : (row + 1) * nx] = low
    m_high, m_low = split(matrix[...])
    width = nz * nx
    for y in range(ny):
        cols = slice(y * width, (y + 1) * width)
        high = highs[:, cols]
        turn[:, cols] = (
            jnp.dot(m_high, high, preferred_element_type=jnp.float32)
            + jnp.dot(m_low, high, preferred_element_type=jnp.float32)
            + jnp.dot(m_high, lows[:, cols], preferred_element_type=jnp.float32)
        )
    tile = (8, nx)
    lane = lax.broadcasted_iota(jnp.int32, tile, 1)
    first_lane = lane == 0
    last_lane = lane == nx - 1
    for part in range(half // 8):
        rows = pl.ds(part * 8, 8)
        tab = table[rows, :]
        rest_speed = column(tab, 0, tile)
        speed_x = column(tab, 1, tile)
        speed_y = column(tab, 2, tile)
        speed_z = column(tab, 3, tile)
        rising_x = column(tab, 4, tile) > 0
        rising_y = column(tab, 5, tile) > 0
        for y in range(ny):
            ps = [full[0, z, y + 1, rows, :] for z in range(nz)]
            ns = [full[1, z, y + 1, rows, :] for z in range(nz)]
            for z in range(nz):
                row = y * nz + z
                p, n = ps[z], ns[z]
                u = jnp.where(rising_x, p, n)
                v = jnp.where(rising_x, n, p)
                u = jnp.where(first_lane, 0.0, pltpu.roll(u, 1, 1))
                v = jnp.where(last_lane, 0.0, pltpu.roll(v, nx - 1, 1))
                angular = turn[rows, row * nx : (row + 1) * nx]
                new_p = rest_speed * p + speed_x * jnp.where(rising_x, u, v) + angular
                new_n = rest_speed * n + speed_x * jnp.where(rising_x, v, u) + angular
                new_p = new_p + speed_y * jnp.where(
                    rising_y, full[0, z, y, rows, :], full[0, z, y + 2, rows, :]
                )
                new_n = new_n + speed_y * jnp.where(
                    rising_y, full[1, z, y + 2, rows, :], full[1, z, y, rows, :]
                )
                if z > 0:
                    new_p = new_p + speed_z * ps[z - 1]
                if z < nz - 1:
                    new_n = new_n + speed_z * ns[z + 1]
                if z < nz - 1:
                    new_rest[0, z, y, rows, :] = new_p
                else:
                    top = new_p
                if z > 0:
                    new_rest[1, z - 1, y, rows, :] = new_n
                else:
                    bottom = new_n
            new_even[y, rows, :] = jnp.where(even, top, bottom)
            new_odd[y, rows, :] = jnp.where(even, bottom, top)


def close_body(plan, table, even_ref, odd_ref, rest_ref, *refs):
    got, (field, held, sems) = refs[:-3], refs[-3:]
    copies = field_copies(plan, held, field, sems)
    even = is_even("gz")
    nz = plan.nz
    size = plan.half // plan.chunks
    for chunk in range(plan.chunks):
        start = chunk * size
        rows = pl.ds(start, size)
        tab = table[rows, :]
        rising_z = column(tab, 6, (size, plan.nx)) > 0
        speed_z = column(tab, 3, (size, plan.nx))
        for y in range(plan.ny):
            arrived = [g[y, rows, :] for g in got]
            low = speed_z * from_below(even, arrived)
            high = speed_z * from_above(even, arrived)
            one, two = even_ref[y, rows, :], odd_ref[y, rows, :]
            for z in range(nz):
                if z == nz - 1:
                    p = jnp.where(even, one, two)
                else:
                    p = rest_ref[0, z, y, rows, :]
                if z == 0:
                    n = jnp.where(even, two, one)
                else:
                    n = rest_ref[1, z - 1, y, rows, :]
                if z == 0:
                    p = p + low
                if z == nz - 1:
                    n = n + high
                base = start * plan.rows + y * nz + z
                held[pl.ds(base, size, stride=plan.rows), :] = jnp.where(rising_z, p, n)
                base = base + plan.half * plan.rows
                held[pl.ds(base, size, stride=plan.rows), :] = jnp.where(rising_z, n, p)
        copies[2 * chunk].start()
        copies[2 * chunk + 1].start()
    for copy in copies:
        copy.wait()


def stay(value):
    return pltpu.with_memory_space_constraint(value, pltpu.HBM)


def call(body, outs, args, scratch=(), raw_in=(), raw_out=False):
    in_specs = []
    for i in range(len(args)):
        in_specs.append(pl.BlockSpec(memory_space=pltpu.HBM if i in raw_in else VMEM))
    moved = sum(math.prod(a.shape) * 4 for a in list(args) + list(outs))
    return pl.pallas_call(
        body,
        out_shape=outs,
        in_specs=in_specs,
        out_specs=[pl.BlockSpec(memory_space=pltpu.HBM if raw_out else VMEM)] * len(outs),
        scratch_shapes=list(scratch),
        cost_estimate=pl.CostEstimate(flops=8 * moved, bytes_accessed=moved, transcendentals=0),
        compiler_params=pltpu.CompilerParams(vmem_limit_bytes=32 << 20),
    )(*args)


def shards(fodf, directions, signs):
    plan = Plan(fodf.shape, lax.axis_size("gz"), lax.axis_size("gy"))
    half = plan.half
    field = fodf.reshape(plan.field.shape)
    edge_outs = [plan.edge] * (1 + plan.y_two)
    state_outs = [plan.layer, plan.layer, plan.rest]
    streamed = [
        VMEM(plan.field.shape, jnp.float32),
        pltpu.SemaphoreType.DMA((plan.chunks, 2)),
    ]
    state = call(
        functools.partial(send_body, plan),
        [plan.layer, plan.layer, plan.rest],
        [stay(signs), stay(field)],
        [VMEM(signs.shape, signs.dtype), *streamed, pltpu.SemaphoreType.DMA],
        raw_in=(0, 1),
    )
    signs, directions, *state = lax.optimization_barrier((signs, directions, *state))
    near = directions[:, :half]
    turn = signs[:, :half].astype(jnp.float32)
    speeds = TIME_STEP * jnp.abs(near)
    columns = jnp.concatenate(
        [1.0 - jnp.sum(speeds, 0, keepdims=True), speeds, turn[:2] * turn[2:], turn[2:]], 0
    )
    table = columns.T
    matrix = angular_matrix(near)
    got = []
    for step in range(ITERS):
        edges = call(
            functools.partial(edge_body, plan, step == 0), edge_outs, [table, *state, *got]
        )
        arriving = exchange(state[0], state[1], "gz")
        y_got = exchange(edges[0], edges[-1], "gy")
        state = call(
            functools.partial(step_body, plan, step == 0),
            state_outs,
            [table, matrix, *state, *got, *y_got],
            [
                VMEM((2, plan.nz, plan.ny + 2, half, plan.nx), jnp.float32),
                VMEM((half, plan.rows * plan.nx), jnp.bfloat16),
                VMEM((half, plan.rows * plan.nx), jnp.bfloat16),
                VMEM((half, plan.rows * plan.nx), jnp.float32),
            ],
        )
        got = arriving
    field = call(
        functools.partial(close_body, plan),
        [plan.field],
        [table, *state, *got],
        streamed,
        raw_out=True,
    )[0]
    return field.reshape(fodf.shape)


def solution(mesh):
    placed = (P(None, "gy", "gz", None), P(), P())
    return jax.shard_map(
        shards, mesh=mesh, in_specs=placed, out_specs=P(None, "gy", "gz", None), check_vma=False
    )
```

```python
import functools
import math

import jax
import jax.numpy as jnp
from jax import lax
from jax.experimental import pallas as pl
from jax.experimental.pallas import tpu as pltpu
from jax.sharding import PartitionSpec as P


LMAX = 8
ITERS = 4
TIME_STEP = 0.5
DIFFUSION = 0.02

VMEM = pltpu.VMEM


def double_factorial(value):
    result = 1
    while value > 1:
        result = result * value
        value = value - 2
    return result


def harmonic_rows(directions):
    along_x, along_y, along_z = (directions[0], directions[1], directions[2])
    cosines = [jnp.ones_like(along_x)]
    sines = [jnp.zeros_like(along_x)]
    for _ in range(1, LMAX + 1):
        cosines.append(cosines[-1] * along_x - sines[-1] * along_y)
        sines.append(cosines[-2] * along_y + sines[-1] * along_x)
    legendre = {}
    for order in range(LMAX + 1):
        legendre[order, order] = double_factorial(2 * order - 1) * jnp.ones_like(along_z)
        if order + 1 <= LMAX:
            legendre[order + 1, order] = (2 * order + 1) * along_z * legendre[order, order]
        for degree in range(order + 2, LMAX + 1):
            legendre[degree, order] = (
                (2 * degree - 1) * along_z * legendre[degree - 1, order]
                - (degree + order - 1) * legendre[degree - 2, order]
            ) / (degree - order)
    basis_rows = []
    eigen_values = []
    for degree in range(0, LMAX + 1, 2):
        for order in range(degree + 1):
            weight_norm = math.sqrt(
                (2 * degree + 1) * math.factorial(degree - order) / math.factorial(degree + order)
            )
            basis_rows.append(weight_norm * legendre[degree, order] * cosines[order])
            eigen_values.append(-float(degree * (degree + 1)))
            if order > 0:
                basis_rows.append(weight_norm * legendre[degree, order] * sines[order])
                eigen_values.append(-float(degree * (degree + 1)))
    return (jnp.stack(basis_rows, 0), jnp.array(eigen_values, dtype=directions.dtype))


def angular_matrix(half):
    basis, eigen_values = harmonic_rows(half)
    gram = 2.0 * jnp.dot(basis, basis.T, precision=lax.Precision.HIGHEST)
    chol_lower = lax.linalg.cholesky(gram, symmetrize_input=False)
    scaled = (TIME_STEP * DIFFUSION * eigen_values)[:, None] * basis
    solved = lax.linalg.triangular_solve(
        chol_lower, jnp.concatenate([basis, scaled], 1), left_side=True, lower=True
    )
    size = basis.shape[1]
    return jnp.dot(solved[:, size:].T, solved[:, :size], precision=lax.Precision.HIGHEST)


def exchange(even_load, odd_load, axis):
    peers = lax.axis_size(axis)
    first = [(i, i ^ 1) for i in range(peers)]
    second = [(i, i + 1 if i % 2 else i - 1) for i in range(1, peers - 1)]
    got = [lax.ppermute(even_load, axis, first)]
    if second:
        got.append(lax.ppermute(odd_load, axis, second))
    return got


class Plan:
    def __init__(self, shape, z_peers, y_peers):
        self.kk, self.ny, self.nz, self.nx = shape
        self.half = self.kk // 2
        self.rows = self.ny * self.nz
        self.chunks = 3
        self.z_two = z_peers > 2
        self.y_two = y_peers > 2
        self.layer = jax.ShapeDtypeStruct((self.ny, self.half, self.nx), jnp.float32)
        self.rest = jax.ShapeDtypeStruct((2, self.nz - 1, self.ny, self.half, self.nx), jnp.float32)
        self.edge = jax.ShapeDtypeStruct((self.nz, self.half, self.nx), jnp.float32)
        self.field = jax.ShapeDtypeStruct((self.kk * self.rows, self.nx), jnp.float32)


def is_even(axis):
    return lax.rem(lax.axis_index(axis), 2) == 0


def column(table, index, shape):
    return jnp.broadcast_to(table[:, index : index + 1], shape)


def from_below(even, got):
    first = got[0]
    if len(got) == 1:
        return jnp.where(even, jnp.zeros_like(first), first)
    return jnp.where(even, got[1], first)


def from_above(even, got):
    first = got[0]
    if len(got) == 1:
        return jnp.where(even, first, jnp.zeros_like(first))
    return jnp.where(even, first, got[1])


def write_edges(even, rising_y, get_p, get_n, plan, outs):
    for z in range(plan.nz):
        top, low = plan.ny - 1, 0
        up = jnp.where(rising_y, get_p(z, top), get_n(z, top))
        down = jnp.where(rising_y, get_n(z, low), get_p(z, low))
        outs[0][z] = jnp.where(even, up, down)
        if plan.y_two:
            outs[1][z] = jnp.where(even, down, up)


def row_to_column(row, size):
    square = jnp.broadcast_to(row, (size, size))
    same = lax.broadcasted_iota(jnp.int32, (size, size), 0) == lax.broadcasted_iota(
        jnp.int32, (size, size), 1
    )
    return jnp.sum(jnp.where(same, square, 0.0), axis=1, keepdims=True)


def field_copies(plan, source, target, sems):
    copies = []
    depth = plan.half // plan.chunks * plan.rows
    for chunk in range(plan.chunks):
        for member in range(2):
            where = pl.ds((member * plan.chunks + chunk) * depth, depth)
            copies.append(
                pltpu.make_async_copy(source.at[where], target.at[where], sems.at[chunk, member])
            )
    return copies


def load_pair(plan, held, start, size, row):
    pair = []
    for member in range(2):
        base = (member * plan.half + start) * plan.rows + row
        pair.append(held[pl.ds(base, size, stride=plan.rows), :])
    return pair


def send_body(plan, signs_raw, field_raw, even_ref, odd_ref, rest_ref, signs, field, sems, small):
    fetch = pltpu.make_async_copy(signs_raw, signs, small)
    fetch.start()
    copies = field_copies(plan, field_raw, field, sems)
    for copy in copies:
        copy.start()
    fetch.wait()
    even = is_even("gz")
    signs_z = signs[2:3, : plan.half].astype(jnp.float32)
    turn = jnp.broadcast_to(row_to_column(signs_z, plan.half), (plan.half, plan.nx))
    size = plan.half // plan.chunks
    for chunk in range(plan.chunks):
        copies[2 * chunk].wait()
        copies[2 * chunk + 1].wait()
        start = chunk * size
        rising_z = turn[start : start + size] > 0
        rows = pl.ds(start, size)
        for y in range(plan.ny):
            for z in range(plan.nz):
                a, b = load_pair(plan, field, start, size, y * plan.nz + z)
                p = jnp.where(rising_z, a, b)
                n = jnp.where(rising_z, b, a)
                if z < plan.nz - 1:
                    rest_ref[0, z, y, rows, :] = p
                else:
                    top = p
                if z > 0:
                    rest_ref[1, z - 1, y, rows, :] = n
                else:
                    bottom = n
            even_ref[y, rows, :] = jnp.where(even, top, bottom)
            odd_ref[y, rows, :] = jnp.where(even, bottom, top)


def member_reader(plan, even, state, got, speed_z):
    even_ref, odd_ref, rest_ref = state

    def get_p(z, y):
        if z == plan.nz - 1:
            return jnp.where(even, even_ref[y], odd_ref[y])
        value = rest_ref[0, z, y]
        if got is not None and z == 0:
            value = value + speed_z * from_below(even, [g[y] for g in got])
        return value

    def get_n(z, y):
        if z == 0:
            return jnp.where(even, odd_ref[y], even_ref[y])
        value = rest_ref[1, z - 1, y]
        if got is not None and z == plan.nz - 1:
            value = value + speed_z * from_above(even, [g[y] for g in got])
        return value

    return get_p, get_n


def edge_body(plan, first, table, even_ref, odd_ref, rest_ref, *refs):
    count = 0 if first else 1 + plan.z_two
    got, edges = refs[:count] or None, refs[count:]
    shape = (plan.half, plan.nx)
    get_p, get_n = member_reader(
        plan, is_even("gz"), (even_ref, odd_ref, rest_ref), got, column(table, 3, shape)
    )
    write_edges(is_even("gy"), column(table, 5, shape) > 0, get_p, get_n, plan, edges)


def split(value):
    high = value.astype(jnp.bfloat16)
    low = (value - high.astype(jnp.float32)).astype(jnp.bfloat16)
    return high, low


def step_body(plan, first, table, matrix, even_ref, odd_ref, rest_ref, *refs):
    z_count = 0 if first else 1 + plan.z_two
    y_count = 1 + plan.y_two
    got = None if first else refs[:z_count]
    y_got = refs[z_count : z_count + y_count]
    new_even, new_odd, new_rest, full, highs, lows, turn = refs[z_count + y_count :]
    half, nx, ny, nz = plan.half, plan.nx, plan.ny, plan.nz
    even = is_even("gz")
    y_even = is_even("gy")
    for part in range(half // 16):
        rows = pl.ds(part * 16, 16)
        speed_z = column(table[rows, :], 3, (16, nx))
        for z in range(nz):
            low = from_below(y_even, [g[z, rows, :] for g in y_got])
            high = from_above(y_even, [g[z, rows, :] for g in y_got])
            full[0, z, 0, rows, :] = low
            full[1, z, 0, rows, :] = low
            full[0, z, ny + 1, rows, :] = high
            full[1, z, ny + 1, rows, :] = high
        for y in range(ny):
            for z in range(nz):
                if z == nz - 1:
                    p = jnp.where(even, even_ref[y, rows, :], odd_ref[y, rows, :])
                else:
                    p = rest_ref[0, z, y, rows, :]
                    if got is not None and z == 0:
                        p = p + speed_z * from_below(even, [g[y, rows, :] for g in got])
                if z == 0:
                    n = jnp.where(even, odd_ref[y, rows, :], even_ref[y, rows, :])
                else:
                    n = rest_ref[1, z - 1, y, rows, :]
                    if got is not None and z == nz - 1:
                        n = n + speed_z * from_above(even, [g[y, rows, :] for g in got])
                full[0, z, y + 1, rows, :] = p
                full[1, z, y + 1, rows, :] = n
                row = y * nz + z
                high, low = split(p + n)
                highs[rows, row * nx : (row + 1) * nx] = high
                lows[rows, row * nx : (row + 1) * nx] = low
    m_high, m_low = split(matrix[...])
    width = nz * nx
    for y in range(ny):
        cols = slice(y * width, (y + 1) * width)
        high = highs[:, cols]
        turn[:, cols] = (
            jnp.dot(m_high, high, preferred_element_type=jnp.float32)
            + jnp.dot(m_low, high, preferred_element_type=jnp.float32)
            + jnp.dot(m_high, lows[:, cols], preferred_element_type=jnp.float32)
        )
    tile = (8, nx)
    lane = lax.broadcasted_iota(jnp.int32, tile, 1)
    first_lane = lane == 0
    last_lane = lane == nx - 1
    for part in range(half // 8):
        rows = pl.ds(part * 8, 8)
        tab = table[rows, :]
        rest_speed = column(tab, 0, tile)
        speed_x = column(tab, 1, tile)
        speed_y = column(tab, 2, tile)
        speed_z = column(tab, 3, tile)
        rising_x = column(tab, 4, tile) > 0
        rising_y = column(tab, 5, tile) > 0
        for y in range(ny):
            ps = [full[0, z, y + 1, rows, :] for z in range(nz)]
            ns = [full[1, z, y + 1, rows, :] for z in range(nz)]
            for z in range(nz):
                row = y * nz + z
                p, n = ps[z], ns[z]
                u = jnp.where(rising_x, p, n)
                v = jnp.where(rising_x, n, p)
                u = jnp.where(first_lane, 0.0, pltpu.roll(u, 1, 1))
                v = jnp.where(last_lane, 0.0, pltpu.roll(v, nx - 1, 1))
                angular = turn[rows, row * nx : (row + 1) * nx]
                new_p = rest_speed * p + speed_x * jnp.where(rising_x, u, v) + angular
                new_n = rest_speed * n + speed_x * jnp.where(rising_x, v, u) + angular
                new_p = new_p + speed_y * jnp.where(
                    rising_y, full[0, z, y, rows, :], full[0, z, y + 2, rows, :]
                )
                new_n = new_n + speed_y * jnp.where(
                    rising_y, full[1, z, y + 2, rows, :], full[1, z, y, rows, :]
                )
                if z > 0:
                    new_p = new_p + speed_z * ps[z - 1]
                if z < nz - 1:
                    new_n = new_n + speed_z * ns[z + 1]
                if z < nz - 1:
                    new_rest[0, z, y, rows, :] = new_p
                else:
                    top = new_p
                if z > 0:
                    new_rest[1, z - 1, y, rows, :] = new_n
                else:
                    bottom = new_n
            new_even[y, rows, :] = jnp.where(even, top, bottom)
            new_odd[y, rows, :] = jnp.where(even, bottom, top)


def close_body(plan, table, even_ref, odd_ref, rest_ref, *refs):
    got, (field, held, sems) = refs[:-3], refs[-3:]
    copies = field_copies(plan, held, field, sems)
    even = is_even("gz")
    nz = plan.nz
    size = plan.half // plan.chunks
    for chunk in range(plan.chunks):
        start = chunk * size
        rows = pl.ds(start, size)
        tab = table[rows, :]
        rising_z = column(tab, 6, (size, plan.nx)) > 0
        speed_z = column(tab, 3, (size, plan.nx))
        for y in range(plan.ny):
            arrived = [g[y, rows, :] for g in got]
            low = speed_z * from_below(even, arrived)
            high = speed_z * from_above(even, arrived)
            one, two = even_ref[y, rows, :], odd_ref[y, rows, :]
            for z in range(nz):
                if z == nz - 1:
                    p = jnp.where(even, one, two)
                else:
                    p = rest_ref[0, z, y, rows, :]
                if z == 0:
                    n = jnp.where(even, two, one)
                else:
                    n = rest_ref[1, z - 1, y, rows, :]
                if z == 0:
                    p = p + low
                if z == nz - 1:
                    n = n + high
                base = start * plan.rows + y * nz + z
                held[pl.ds(base, size, stride=plan.rows), :] = jnp.where(rising_z, p, n)
                base = base + plan.half * plan.rows
                held[pl.ds(base, size, stride=plan.rows), :] = jnp.where(rising_z, n, p)
        copies[2 * chunk].start()
        copies[2 * chunk + 1].start()
    for copy in copies:
        copy.wait()


def stay(value):
    return pltpu.with_memory_space_constraint(value, pltpu.HBM)


def call(body, outs, args, scratch=(), raw_in=(), raw_out=False):
    in_specs = []
    for i in range(len(args)):
        in_specs.append(pl.BlockSpec(memory_space=pltpu.HBM if i in raw_in else VMEM))
    moved = sum(math.prod(a.shape) * 4 for a in list(args) + list(outs))
    return pl.pallas_call(
        body,
        out_shape=outs,
        in_specs=in_specs,
        out_specs=[pl.BlockSpec(memory_space=pltpu.HBM if raw_out else VMEM)] * len(outs),
        scratch_shapes=list(scratch),
        cost_estimate=pl.CostEstimate(flops=8 * moved, bytes_accessed=moved, transcendentals=0),
        compiler_params=pltpu.CompilerParams(vmem_limit_bytes=32 << 20),
    )(*args)


def shards(fodf, directions, signs):
    plan = Plan(fodf.shape, lax.axis_size("gz"), lax.axis_size("gy"))
    half = plan.half
    field = fodf.reshape(plan.field.shape)
    edge_outs = [plan.edge] * (1 + plan.y_two)
    state_outs = [plan.layer, plan.layer, plan.rest]
    streamed = [
        VMEM(plan.field.shape, jnp.float32),
        pltpu.SemaphoreType.DMA((plan.chunks, 2)),
    ]
    state = call(
        functools.partial(send_body, plan),
        [plan.layer, plan.layer, plan.rest],
        [stay(signs), stay(field)],
        [VMEM(signs.shape, signs.dtype), *streamed, pltpu.SemaphoreType.DMA],
        raw_in=(0, 1),
    )
    signs, directions, *state = lax.optimization_barrier((signs, directions, *state))
    near = directions[:, :half]
    turn = signs[:, :half].astype(jnp.float32)
    speeds = TIME_STEP * jnp.abs(near)
    columns = jnp.concatenate(
        [1.0 - jnp.sum(speeds, 0, keepdims=True), speeds, turn[:2] * turn[2:], turn[2:]], 0
    )
    table = columns.T
    matrix = angular_matrix(near)
    got = []
    for step in range(ITERS):
        edges = call(
            functools.partial(edge_body, plan, step == 0), edge_outs, [table, *state, *got]
        )
        arriving = exchange(state[0], state[1], "gz")
        y_got = exchange(edges[0], edges[-1], "gy")
        state = call(
            functools.partial(step_body, plan, step == 0),
            state_outs,
            [table, matrix, *state, *got, *y_got],
            [
                VMEM((2, plan.nz, plan.ny + 2, half, plan.nx), jnp.float32),
                VMEM((half, plan.rows * plan.nx), jnp.bfloat16),
                VMEM((half, plan.rows * plan.nx), jnp.bfloat16),
                VMEM((half, plan.rows * plan.nx), jnp.float32),
            ],
        )
        got = arriving
    field = call(
        functools.partial(close_body, plan),
        [plan.field],
        [table, *state, *got],
        streamed,
        raw_out=True,
    )[0]
    return field.reshape(fodf.shape)


def solution(mesh):
    placed = (P(None, "gy", "gz", None), P(), P())
    return jax.shard_map(
        shards, mesh=mesh, in_specs=placed, out_specs=P(None, "gy", "gz", None), check_vma=False
    )
```

```python
import functools
import math

import jax
import jax.numpy as jnp
from jax import lax
from jax.experimental import pallas as pl
from jax.experimental.pallas import tpu as pltpu
from jax.sharding import PartitionSpec as P


LMAX = 8
ITERS = 4
TIME_STEP = 0.5
DIFFUSION = 0.02

VMEM = pltpu.VMEM


def double_factorial(value):
    result = 1
    while value > 1:
        result = result * value
        value = value - 2
    return result


def harmonic_rows(directions):
    along_x, along_y, along_z = (directions[0], directions[1], directions[2])
    cosines = [jnp.ones_like(along_x)]
    sines = [jnp.zeros_like(along_x)]
    for _ in range(1, LMAX + 1):
        cosines.append(cosines[-1] * along_x - sines[-1] * along_y)
        sines.append(cosines[-2] * along_y + sines[-1] * along_x)
    legendre = {}
    for order in range(LMAX + 1):
        legendre[order, order] = double_factorial(2 * order - 1) * jnp.ones_like(along_z)
        if order + 1 <= LMAX:
            legendre[order + 1, order] = (2 * order + 1) * along_z * legendre[order, order]
        for degree in range(order + 2, LMAX + 1):
            legendre[degree, order] = (
                (2 * degree - 1) * along_z * legendre[degree - 1, order]
                - (degree + order - 1) * legendre[degree - 2, order]
            ) / (degree - order)
    basis_rows = []
    eigen_values = []
    for degree in range(0, LMAX + 1, 2):
        for order in range(degree + 1):
            weight_norm = math.sqrt(
                (2 * degree + 1) * math.factorial(degree - order) / math.factorial(degree + order)
            )
            basis_rows.append(weight_norm * legendre[degree, order] * cosines[order])
            eigen_values.append(-float(degree * (degree + 1)))
            if order > 0:
                basis_rows.append(weight_norm * legendre[degree, order] * sines[order])
                eigen_values.append(-float(degree * (degree + 1)))
    return (jnp.stack(basis_rows, 0), jnp.array(eigen_values, dtype=directions.dtype))


def angular_matrix(half):
    basis, eigen_values = harmonic_rows(half)
    gram = 2.0 * jnp.dot(basis, basis.T, precision=lax.Precision.HIGHEST)
    chol_lower = lax.linalg.cholesky(gram, symmetrize_input=False)
    scaled = (TIME_STEP * DIFFUSION * eigen_values)[:, None] * basis
    return call(
        functools.partial(solve_body, basis.shape[0]),
        [jax.ShapeDtypeStruct((basis.shape[1],) * 2, jnp.float32)],
        [padded(chol_lower), padded(scaled), padded(basis)],
    )[0]


def padded(value):
    return jnp.pad(value, ((0, -value.shape[0] % 8), (0, 0)))


def solve_body(count, chol, left, right, out):
    size, width = left.shape
    factor = chol[...]
    row = lax.broadcasted_iota(jnp.int32, factor.shape, 0)
    col = lax.broadcasted_iota(jnp.int32, factor.shape, 1)
    diagonal = jnp.where(row == col, factor, 0.0)
    by_lane = jnp.sum(diagonal, axis=0, keepdims=True)
    factor = jnp.where(row > col, factor / by_lane, 0.0)
    weight = jnp.sum(diagonal, axis=1, keepdims=True)
    weight = jnp.where(weight == 0.0, 1.0, weight)
    blocks = [
        [ref[8 * block : 8 * block + 8, :] for block in range(size // 8)] for ref in (left, right)
    ]
    for j in range(count):
        home, place = divmod(j, 8)
        pivots = [jnp.broadcast_to(side[home][place : place + 1, :], (8, width)) for side in blocks]
        for block in range(home, size // 8):
            ratio = jnp.broadcast_to(factor[8 * block : 8 * block + 8, j : j + 1], (8, width))
            for side, pivot in zip(blocks, pivots):
                side[block] = side[block] - ratio * pivot
    first, second = (jnp.concatenate(side, 0) for side in blocks)
    out[...] = lax.dot_general(
        first,
        second / (weight * weight),
        (((0,), (0,)), ((), ())),
        precision=lax.Precision.HIGHEST,
        preferred_element_type=jnp.float32,
    )


def exchange(even_load, odd_load, axis):
    peers = lax.axis_size(axis)
    first = [(i, i ^ 1) for i in range(peers)]
    second = [(i, i + 1 if i % 2 else i - 1) for i in range(1, peers - 1)]
    got = [lax.ppermute(even_load, axis, first)]
    if second:
        got.append(lax.ppermute(odd_load, axis, second))
    return got


class Plan:
    def __init__(self, shape, z_peers, y_peers):
        self.kk, self.ny, self.nz, self.nx = shape
        self.half = self.kk // 2
        self.rows = self.ny * self.nz
        self.chunks = 3
        self.z_two = z_peers > 2
        self.y_two = y_peers > 2
        self.layer = jax.ShapeDtypeStruct((self.ny, self.half, self.nx), jnp.float32)
        self.rest = jax.ShapeDtypeStruct((2, self.nz - 1, self.ny, self.half, self.nx), jnp.float32)
        self.edge = jax.ShapeDtypeStruct((self.nz, self.half, self.nx), jnp.float32)
        self.field = jax.ShapeDtypeStruct((self.kk * self.rows, self.nx), jnp.float32)


def is_even(axis):
    return lax.rem(lax.axis_index(axis), 2) == 0


def column(table, index, shape):
    return jnp.broadcast_to(table[:, index : index + 1], shape)


def from_below(even, got):
    first = got[0]
    if len(got) == 1:
        return jnp.where(even, jnp.zeros_like(first), first)
    return jnp.where(even, got[1], first)


def from_above(even, got):
    first = got[0]
    if len(got) == 1:
        return jnp.where(even, first, jnp.zeros_like(first))
    return jnp.where(even, first, got[1])


def write_edges(even, rising_y, get_p, get_n, plan, outs):
    for z in range(plan.nz):
        top, low = plan.ny - 1, 0
        up = jnp.where(rising_y, get_p(z, top), get_n(z, top))
        down = jnp.where(rising_y, get_n(z, low), get_p(z, low))
        outs[0][z] = jnp.where(even, up, down)
        if plan.y_two:
            outs[1][z] = jnp.where(even, down, up)


def row_to_column(row, size):
    square = jnp.broadcast_to(row, (size, size))
    same = lax.broadcasted_iota(jnp.int32, (size, size), 0) == lax.broadcasted_iota(
        jnp.int32, (size, size), 1
    )
    return jnp.sum(jnp.where(same, square, 0.0), axis=1, keepdims=True)


def field_copies(plan, source, target, sems):
    copies = []
    depth = plan.half // plan.chunks * plan.rows
    for chunk in range(plan.chunks):
        for member in range(2):
            where = pl.ds((member * plan.chunks + chunk) * depth, depth)
            copies.append(
                pltpu.make_async_copy(source.at[where], target.at[where], sems.at[chunk, member])
            )
    return copies


def load_pair(plan, held, start, size, row):
    pair = []
    for member in range(2):
        base = (member * plan.half + start) * plan.rows + row
        pair.append(held[pl.ds(base, size, stride=plan.rows), :])
    return pair


def send_body(plan, signs_raw, field_raw, even_ref, odd_ref, rest_ref, signs, field, sems, small):
    fetch = pltpu.make_async_copy(signs_raw, signs, small)
    fetch.start()
    copies = field_copies(plan, field_raw, field, sems)
    for copy in copies:
        copy.start()
    fetch.wait()
    even = is_even("gz")
    signs_z = signs[2:3, : plan.half].astype(jnp.float32)
    turn = jnp.broadcast_to(row_to_column(signs_z, plan.half), (plan.half, plan.nx))
    size = plan.half // plan.chunks
    for chunk in range(plan.chunks):
        copies[2 * chunk].wait()
        copies[2 * chunk + 1].wait()
        start = chunk * size
        rising_z = turn[start : start + size] > 0
        rows = pl.ds(start, size)
        for y in range(plan.ny):
            for z in range(plan.nz):
                a, b = load_pair(plan, field, start, size, y * plan.nz + z)
                p = jnp.where(rising_z, a, b)
                n = jnp.where(rising_z, b, a)
                if z < plan.nz - 1:
                    rest_ref[0, z, y, rows, :] = p
                else:
                    top = p
                if z > 0:
                    rest_ref[1, z - 1, y, rows, :] = n
                else:
                    bottom = n
            even_ref[y, rows, :] = jnp.where(even, top, bottom)
            odd_ref[y, rows, :] = jnp.where(even, bottom, top)


def member_reader(plan, even, state, got, speed_z):
    even_ref, odd_ref, rest_ref = state

    def get_p(z, y):
        if z == plan.nz - 1:
            return jnp.where(even, even_ref[y], odd_ref[y])
        value = rest_ref[0, z, y]
        if got is not None and z == 0:
            value = value + speed_z * from_below(even, [g[y] for g in got])
        return value

    def get_n(z, y):
        if z == 0:
            return jnp.where(even, odd_ref[y], even_ref[y])
        value = rest_ref[1, z - 1, y]
        if got is not None and z == plan.nz - 1:
            value = value + speed_z * from_above(even, [g[y] for g in got])
        return value

    return get_p, get_n


def edge_body(plan, first, table, even_ref, odd_ref, rest_ref, *refs):
    count = 0 if first else 1 + plan.z_two
    got, edges = refs[:count] or None, refs[count:]
    shape = (plan.half, plan.nx)
    get_p, get_n = member_reader(
        plan, is_even("gz"), (even_ref, odd_ref, rest_ref), got, column(table, 3, shape)
    )
    write_edges(is_even("gy"), column(table, 5, shape) > 0, get_p, get_n, plan, edges)


def split(value):
    high = value.astype(jnp.bfloat16)
    low = (value - high.astype(jnp.float32)).astype(jnp.bfloat16)
    return high, low


def step_body(plan, first, table, matrix, even_ref, odd_ref, rest_ref, *refs):
    z_count = 0 if first else 1 + plan.z_two
    y_count = 1 + plan.y_two
    got = None if first else refs[:z_count]
    y_got = refs[z_count : z_count + y_count]
    new_even, new_odd, new_rest, full, highs, lows, turn = refs[z_count + y_count :]
    half, nx, ny, nz = plan.half, plan.nx, plan.ny, plan.nz
    even = is_even("gz")
    y_even = is_even("gy")
    for part in range(half // 16):
        rows = pl.ds(part * 16, 16)
        speed_z = column(table[rows, :], 3, (16, nx))
        for z in range(nz):
            low = from_below(y_even, [g[z, rows, :] for g in y_got])
            high = from_above(y_even, [g[z, rows, :] for g in y_got])
            full[0, z, 0, rows, :] = low
            full[1, z, 0, rows, :] = low
            full[0, z, ny + 1, rows, :] = high
            full[1, z, ny + 1, rows, :] = high
        for y in range(ny):
            for z in range(nz):
                if z == nz - 1:
                    p = jnp.where(even, even_ref[y, rows, :], odd_ref[y, rows, :])
                else:
                    p = rest_ref[0, z, y, rows, :]
                    if got is not None and z == 0:
                        p = p + speed_z * from_below(even, [g[y, rows, :] for g in got])
                if z == 0:
                    n = jnp.where(even, odd_ref[y, rows, :], even_ref[y, rows, :])
                else:
                    n = rest_ref[1, z - 1, y, rows, :]
                    if got is not None and z == nz - 1:
                        n = n + speed_z * from_above(even, [g[y, rows, :] for g in got])
                full[0, z, y + 1, rows, :] = p
                full[1, z, y + 1, rows, :] = n
                row = y * nz + z
                high, low = split(p + n)
                highs[rows, row * nx : (row + 1) * nx] = high
                lows[rows, row * nx : (row + 1) * nx] = low
    m_high, m_low = split(matrix[...])
    width = nz * nx
    for y in range(ny):
        cols = slice(y * width, (y + 1) * width)
        high = highs[:, cols]
        turn[:, cols] = (
            jnp.dot(m_high, high, preferred_element_type=jnp.float32)
            + jnp.dot(m_low, high, preferred_element_type=jnp.float32)
            + jnp.dot(m_high, lows[:, cols], preferred_element_type=jnp.float32)
        )
    tile = (8, nx)
    lane = lax.broadcasted_iota(jnp.int32, tile, 1)
    first_lane = lane == 0
    last_lane = lane == nx - 1
    for part in range(half // 8):
        rows = pl.ds(part * 8, 8)
        tab = table[rows, :]
        rest_speed = column(tab, 0, tile)
        speed_x = column(tab, 1, tile)
        speed_y = column(tab, 2, tile)
        speed_z = column(tab, 3, tile)
        rising_x = column(tab, 4, tile) > 0
        rising_y = column(tab, 5, tile) > 0
        for y in range(ny):
            ps = [full[0, z, y + 1, rows, :] for z in range(nz)]
            ns = [full[1, z, y + 1, rows, :] for z in range(nz)]
            for z in range(nz):
                row = y * nz + z
                p, n = ps[z], ns[z]
                u = jnp.where(rising_x, p, n)
                v = jnp.where(rising_x, n, p)
                u = jnp.where(first_lane, 0.0, pltpu.roll(u, 1, 1))
                v = jnp.where(last_lane, 0.0, pltpu.roll(v, nx - 1, 1))
                angular = turn[rows, row * nx : (row + 1) * nx]
                new_p = rest_speed * p + speed_x * jnp.where(rising_x, u, v) + angular
                new_n = rest_speed * n + speed_x * jnp.where(rising_x, v, u) + angular
                new_p = new_p + speed_y * jnp.where(
                    rising_y, full[0, z, y, rows, :], full[0, z, y + 2, rows, :]
                )
                new_n = new_n + speed_y * jnp.where(
                    rising_y, full[1, z, y + 2, rows, :], full[1, z, y, rows, :]
                )
                if z > 0:
                    new_p = new_p + speed_z * ps[z - 1]
                if z < nz - 1:
                    new_n = new_n + speed_z * ns[z + 1]
                if z < nz - 1:
                    new_rest[0, z, y, rows, :] = new_p
                else:
                    top = new_p
                if z > 0:
                    new_rest[1, z - 1, y, rows, :] = new_n
                else:
                    bottom = new_n
            new_even[y, rows, :] = jnp.where(even, top, bottom)
            new_odd[y, rows, :] = jnp.where(even, bottom, top)


def close_body(plan, table, even_ref, odd_ref, rest_ref, *refs):
    got, (field, held, sems) = refs[:-3], refs[-3:]
    copies = field_copies(plan, held, field, sems)
    even = is_even("gz")
    nz = plan.nz
    size = plan.half // plan.chunks
    for chunk in range(plan.chunks):
        start = chunk * size
        rows = pl.ds(start, size)
        tab = table[rows, :]
        rising_z = column(tab, 6, (size, plan.nx)) > 0
        speed_z = column(tab, 3, (size, plan.nx))
        for y in range(plan.ny):
            arrived = [g[y, rows, :] for g in got]
            low = speed_z * from_below(even, arrived)
            high = speed_z * from_above(even, arrived)
            one, two = even_ref[y, rows, :], odd_ref[y, rows, :]
            for z in range(nz):
                if z == nz - 1:
                    p = jnp.where(even, one, two)
                else:
                    p = rest_ref[0, z, y, rows, :]
                if z == 0:
                    n = jnp.where(even, two, one)
                else:
                    n = rest_ref[1, z - 1, y, rows, :]
                if z == 0:
                    p = p + low
                if z == nz - 1:
                    n = n + high
                base = start * plan.rows + y * nz + z
                held[pl.ds(base, size, stride=plan.rows), :] = jnp.where(rising_z, p, n)
                base = base + plan.half * plan.rows
                held[pl.ds(base, size, stride=plan.rows), :] = jnp.where(rising_z, n, p)
        copies[2 * chunk].start()
        copies[2 * chunk + 1].start()
    for copy in copies:
        copy.wait()


def stay(value):
    return pltpu.with_memory_space_constraint(value, pltpu.HBM)


def call(body, outs, args, scratch=(), raw_in=(), raw_out=False):
    in_specs = []
    for i in range(len(args)):
        in_specs.append(pl.BlockSpec(memory_space=pltpu.HBM if i in raw_in else VMEM))
    moved = sum(math.prod(a.shape) * 4 for a in list(args) + list(outs))
    return pl.pallas_call(
        body,
        out_shape=outs,
        in_specs=in_specs,
        out_specs=[pl.BlockSpec(memory_space=pltpu.HBM if raw_out else VMEM)] * len(outs),
        scratch_shapes=list(scratch),
        cost_estimate=pl.CostEstimate(flops=8 * moved, bytes_accessed=moved, transcendentals=0),
        compiler_params=pltpu.CompilerParams(vmem_limit_bytes=32 << 20),
    )(*args)


def shards(fodf, directions, signs):
    plan = Plan(fodf.shape, lax.axis_size("gz"), lax.axis_size("gy"))
    half = plan.half
    field = fodf.reshape(plan.field.shape)
    edge_outs = [plan.edge] * (1 + plan.y_two)
    state_outs = [plan.layer, plan.layer, plan.rest]
    streamed = [
        VMEM(plan.field.shape, jnp.float32),
        pltpu.SemaphoreType.DMA((plan.chunks, 2)),
    ]
    state = call(
        functools.partial(send_body, plan),
        [plan.layer, plan.layer, plan.rest],
        [stay(signs), stay(field)],
        [VMEM(signs.shape, signs.dtype), *streamed, pltpu.SemaphoreType.DMA],
        raw_in=(0, 1),
    )
    signs, directions, *state = lax.optimization_barrier((signs, directions, *state))
    near = directions[:, :half]
    turn = signs[:, :half].astype(jnp.float32)
    speeds = TIME_STEP * jnp.abs(near)
    columns = jnp.concatenate(
        [1.0 - jnp.sum(speeds, 0, keepdims=True), speeds, turn[:2] * turn[2:], turn[2:]], 0
    )
    table = columns.T
    matrix = angular_matrix(near)
    got = []
    for step in range(ITERS):
        edges = call(
            functools.partial(edge_body, plan, step == 0), edge_outs, [table, *state, *got]
        )
        arriving = exchange(state[0], state[1], "gz")
        y_got = exchange(edges[0], edges[-1], "gy")
        state = call(
            functools.partial(step_body, plan, step == 0),
            state_outs,
            [table, matrix, *state, *got, *y_got],
            [
                VMEM((2, plan.nz, plan.ny + 2, half, plan.nx), jnp.float32),
                VMEM((half, plan.rows * plan.nx), jnp.bfloat16),
                VMEM((half, plan.rows * plan.nx), jnp.bfloat16),
                VMEM((half, plan.rows * plan.nx), jnp.float32),
            ],
        )
        got = arriving
    field = call(
        functools.partial(close_body, plan),
        [plan.field],
        [table, *state, *got],
        streamed,
        raw_out=True,
    )[0]
    return field.reshape(fodf.shape)


def solution(mesh):
    placed = (P(None, "gy", "gz", None), P(), P())
    return jax.shard_map(
        shards, mesh=mesh, in_specs=placed, out_specs=P(None, "gy", "gz", None), check_vma=False
    )
```

```python
import functools
import math

import jax
import jax.numpy as jnp
from jax import lax
from jax.experimental import pallas as pl
from jax.experimental.pallas import tpu as pltpu
from jax.sharding import PartitionSpec as P


LMAX = 8
ITERS = 4
TIME_STEP = 0.5
DIFFUSION = 0.02

PIECES = 2
VMEM = pltpu.VMEM


def double_factorial(value):
    result = 1
    while value > 1:
        result = result * value
        value = value - 2
    return result


def harmonic_rows(directions):
    along_x, along_y, along_z = (directions[0], directions[1], directions[2])
    cosines = [jnp.ones_like(along_x)]
    sines = [jnp.zeros_like(along_x)]
    for _ in range(1, LMAX + 1):
        cosines.append(cosines[-1] * along_x - sines[-1] * along_y)
        sines.append(cosines[-2] * along_y + sines[-1] * along_x)
    legendre = {}
    for order in range(LMAX + 1):
        legendre[order, order] = double_factorial(2 * order - 1) * jnp.ones_like(along_z)
        if order + 1 <= LMAX:
            legendre[order + 1, order] = (2 * order + 1) * along_z * legendre[order, order]
        for degree in range(order + 2, LMAX + 1):
            legendre[degree, order] = (
                (2 * degree - 1) * along_z * legendre[degree - 1, order]
                - (degree + order - 1) * legendre[degree - 2, order]
            ) / (degree - order)
    basis_rows = []
    eigen_values = []
    for degree in range(0, LMAX + 1, 2):
        for order in range(degree + 1):
            weight_norm = math.sqrt(
                (2 * degree + 1) * math.factorial(degree - order) / math.factorial(degree + order)
            )
            basis_rows.append(weight_norm * legendre[degree, order] * cosines[order])
            eigen_values.append(-float(degree * (degree + 1)))
            if order > 0:
                basis_rows.append(weight_norm * legendre[degree, order] * sines[order])
                eigen_values.append(-float(degree * (degree + 1)))
    return (jnp.stack(basis_rows, 0), jnp.array(eigen_values, dtype=directions.dtype))


def angular_matrix(half):
    basis, eigen_values = harmonic_rows(half)
    gram = 2.0 * jnp.dot(basis, basis.T, precision=lax.Precision.HIGHEST)
    chol_lower = lax.linalg.cholesky(gram, symmetrize_input=False)
    scaled = (TIME_STEP * DIFFUSION * eigen_values)[:, None] * basis
    return call(
        functools.partial(solve_body, basis.shape[0]),
        [jax.ShapeDtypeStruct((basis.shape[1],) * 2, jnp.float32)],
        [padded(chol_lower), padded(scaled), padded(basis)],
    )[0]


def padded(value):
    return jnp.pad(value, ((0, -value.shape[0] % 8), (0, 0)))


def solve_body(count, chol, left, right, out):
    size, width = left.shape
    factor = chol[...]
    row = lax.broadcasted_iota(jnp.int32, factor.shape, 0)
    col = lax.broadcasted_iota(jnp.int32, factor.shape, 1)
    diagonal = jnp.where(row == col, factor, 0.0)
    by_lane = jnp.sum(diagonal, axis=0, keepdims=True)
    factor = jnp.where(row > col, factor / by_lane, 0.0)
    weight = jnp.sum(diagonal, axis=1, keepdims=True)
    weight = jnp.where(weight == 0.0, 1.0, weight)
    blocks = [
        [ref[8 * block : 8 * block + 8, :] for block in range(size // 8)] for ref in (left, right)
    ]
    for j in range(count):
        home, place = divmod(j, 8)
        pivots = [jnp.broadcast_to(side[home][place : place + 1, :], (8, width)) for side in blocks]
        for block in range(home, size // 8):
            ratio = jnp.broadcast_to(factor[8 * block : 8 * block + 8, j : j + 1], (8, width))
            for side, pivot in zip(blocks, pivots):
                side[block] = side[block] - ratio * pivot
    first, second = (jnp.concatenate(side, 0) for side in blocks)
    out[...] = lax.dot_general(
        first,
        second / (weight * weight),
        (((0,), (0,)), ((), ())),
        precision=lax.Precision.HIGHEST,
        preferred_element_type=jnp.float32,
    )


def exchange(even_load, odd_load, axis):
    peers = lax.axis_size(axis)
    first = [(i, i ^ 1) for i in range(peers)]
    second = [(i, i + 1 if i % 2 else i - 1) for i in range(1, peers - 1)]
    got = [lax.ppermute(even_load, axis, first)]
    if second:
        got.append(lax.ppermute(odd_load, axis, second))
    return got


class Plan:
    def __init__(self, shape, z_peers, y_peers):
        self.kk, self.ny, self.nz, self.nx = shape
        self.half = self.kk // 2
        self.rows = self.ny * self.nz
        self.chunks = 3
        self.piece = jax.ShapeDtypeStruct((self.ny, self.half // PIECES, self.nx), jnp.float32)
        self.z_two = z_peers > 2
        self.y_two = y_peers > 2
        self.layer = jax.ShapeDtypeStruct((self.ny, self.half, self.nx), jnp.float32)
        self.rest = jax.ShapeDtypeStruct((2, self.nz - 1, self.ny, self.half, self.nx), jnp.float32)
        self.edge = jax.ShapeDtypeStruct((self.nz, self.half, self.nx), jnp.float32)
        self.field = jax.ShapeDtypeStruct((self.kk * self.rows, self.nx), jnp.float32)


def is_even(axis):
    return lax.rem(lax.axis_index(axis), 2) == 0


def column(table, index, shape):
    return jnp.broadcast_to(table[:, index : index + 1], shape)


def from_below(even, got):
    first = got[0]
    if len(got) == 1:
        return jnp.where(even, jnp.zeros_like(first), first)
    return jnp.where(even, got[1], first)


def from_above(even, got):
    first = got[0]
    if len(got) == 1:
        return jnp.where(even, first, jnp.zeros_like(first))
    return jnp.where(even, first, got[1])


def write_edges(even, rising_y, get_p, get_n, plan, outs):
    for z in range(plan.nz):
        top, low = plan.ny - 1, 0
        up = jnp.where(rising_y, get_p(z, top), get_n(z, top))
        down = jnp.where(rising_y, get_n(z, low), get_p(z, low))
        outs[0][z] = jnp.where(even, up, down)
        if plan.y_two:
            outs[1][z] = jnp.where(even, down, up)


def row_to_column(row, size):
    square = jnp.broadcast_to(row, (size, size))
    same = lax.broadcasted_iota(jnp.int32, (size, size), 0) == lax.broadcasted_iota(
        jnp.int32, (size, size), 1
    )
    return jnp.sum(jnp.where(same, square, 0.0), axis=1, keepdims=True)


def field_copies(plan, source, target, sems, start=0, length=None):
    copies = []
    size = (length or plan.half) // plan.chunks
    depth = size * plan.rows
    for chunk in range(plan.chunks):
        for member in range(2):
            first = member * plan.half + start + chunk * size
            where = pl.ds(first * plan.rows, depth)
            copies.append(
                pltpu.make_async_copy(source.at[where], target.at[where], sems.at[chunk, member])
            )
    return copies


def load_pair(plan, held, start, size, row):
    pair = []
    for member in range(2):
        base = (member * plan.half + start) * plan.rows + row
        pair.append(held[pl.ds(base, size, stride=plan.rows), :])
    return pair


def send_body(plan, signs_raw, field_raw, even_ref, odd_ref, rest_ref, signs, field, sems, small):
    fetch = pltpu.make_async_copy(signs_raw, signs, small)
    fetch.start()
    copies = field_copies(plan, field_raw, field, sems)
    for copy in copies:
        copy.start()
    fetch.wait()
    even = is_even("gz")
    signs_z = signs[2:3, : plan.half].astype(jnp.float32)
    turn = jnp.broadcast_to(row_to_column(signs_z, plan.half), (plan.half, plan.nx))
    size = plan.half // plan.chunks
    for chunk in range(plan.chunks):
        copies[2 * chunk].wait()
        copies[2 * chunk + 1].wait()
        start = chunk * size
        rising_z = turn[start : start + size] > 0
        rows = pl.ds(start, size)
        for y in range(plan.ny):
            for z in range(plan.nz):
                a, b = load_pair(plan, field, start, size, y * plan.nz + z)
                p = jnp.where(rising_z, a, b)
                n = jnp.where(rising_z, b, a)
                if z < plan.nz - 1:
                    rest_ref[0, z, y, rows, :] = p
                else:
                    top = p
                if z > 0:
                    rest_ref[1, z - 1, y, rows, :] = n
                else:
                    bottom = n
            even_ref[y, rows, :] = jnp.where(even, top, bottom)
            odd_ref[y, rows, :] = jnp.where(even, bottom, top)


def state_refs(refs, pieces):
    loads, rest = refs[: 2 * pieces], refs[2 * pieces]
    return loads[0::2], loads[1::2], rest, refs[2 * pieces + 1 :]


def take(refs, y, start, size, half):
    piece, inner = divmod(start, half // len(refs))
    return refs[piece][y, pl.ds(inner, size), :]


def whole(refs, y):
    return jnp.concatenate([ref[y] for ref in refs], 0) if len(refs) > 1 else refs[0][y]


def member_reader(plan, even, state, got, speed_z):
    evens, odds, rest_ref = state

    def get_p(z, y):
        if z == plan.nz - 1:
            return jnp.where(even, whole(evens, y), whole(odds, y))
        value = rest_ref[0, z, y]
        if got is not None and z == 0:
            value = value + speed_z * from_below(even, [g[y] for g in got])
        return value

    def get_n(z, y):
        if z == 0:
            return jnp.where(even, whole(odds, y), whole(evens, y))
        value = rest_ref[1, z - 1, y]
        if got is not None and z == plan.nz - 1:
            value = value + speed_z * from_above(even, [g[y] for g in got])
        return value

    return get_p, get_n


def edge_body(plan, first, split_in, table, *refs):
    evens, odds, rest_ref, refs = state_refs(refs, split_in)
    count = 0 if first else 1 + plan.z_two
    got, edges = refs[:count] or None, refs[count:]
    shape = (plan.half, plan.nx)
    get_p, get_n = member_reader(
        plan, is_even("gz"), (evens, odds, rest_ref), got, column(table, 3, shape)
    )
    write_edges(is_even("gy"), column(table, 5, shape) > 0, get_p, get_n, plan, edges)


def split(value):
    high = value.astype(jnp.bfloat16)
    low = (value - high.astype(jnp.float32)).astype(jnp.bfloat16)
    return high, low


def step_body(plan, first, split_in, pieces, table, matrix, *refs):
    evens, odds, rest_ref, refs = state_refs(refs, split_in)
    z_count = 0 if first else 1 + plan.z_two
    y_count = 1 + plan.y_two
    got = None if first else refs[:z_count]
    y_got = refs[z_count : z_count + y_count]
    outs = refs[z_count + y_count :]
    loads, (new_rest, full, highs, lows, turn) = outs[: 2 * pieces], outs[2 * pieces :]
    half, nx, ny, nz = plan.half, plan.nx, plan.ny, plan.nz
    even = is_even("gz")
    y_even = is_even("gy")
    for part in range(half // 16):
        rows = pl.ds(part * 16, 16)
        speed_z = column(table[rows, :], 3, (16, nx))
        for z in range(nz):
            low = from_below(y_even, [g[z, rows, :] for g in y_got])
            high = from_above(y_even, [g[z, rows, :] for g in y_got])
            full[0, z, 0, rows, :] = low
            full[1, z, 0, rows, :] = low
            full[0, z, ny + 1, rows, :] = high
            full[1, z, ny + 1, rows, :] = high
        for y in range(ny):
            for z in range(nz):
                if z == nz - 1:
                    p = jnp.where(even, take(evens, y, part * 16, 16, half), take(odds, y, part * 16, 16, half))
                else:
                    p = rest_ref[0, z, y, rows, :]
                    if got is not None and z == 0:
                        p = p + speed_z * from_below(even, [g[y, rows, :] for g in got])
                if z == 0:
                    n = jnp.where(even, take(odds, y, part * 16, 16, half), take(evens, y, part * 16, 16, half))
                else:
                    n = rest_ref[1, z - 1, y, rows, :]
                    if got is not None and z == nz - 1:
                        n = n + speed_z * from_above(even, [g[y, rows, :] for g in got])
                full[0, z, y + 1, rows, :] = p
                full[1, z, y + 1, rows, :] = n
                row = y * nz + z
                high, low = split(p + n)
                highs[rows, row * nx : (row + 1) * nx] = high
                lows[rows, row * nx : (row + 1) * nx] = low
    m_high, m_low = split(matrix[...])
    width = nz * nx
    for y in range(ny):
        cols = slice(y * width, (y + 1) * width)
        high = highs[:, cols]
        turn[:, cols] = (
            jnp.dot(m_high, high, preferred_element_type=jnp.float32)
            + jnp.dot(m_low, high, preferred_element_type=jnp.float32)
            + jnp.dot(m_high, lows[:, cols], preferred_element_type=jnp.float32)
        )
    tile = (8, nx)
    lane = lax.broadcasted_iota(jnp.int32, tile, 1)
    first_lane = lane == 0
    last_lane = lane == nx - 1
    for part in range(half // 8):
        rows = pl.ds(part * 8, 8)
        tab = table[rows, :]
        rest_speed = column(tab, 0, tile)
        speed_x = column(tab, 1, tile)
        speed_y = column(tab, 2, tile)
        speed_z = column(tab, 3, tile)
        rising_x = column(tab, 4, tile) > 0
        rising_y = column(tab, 5, tile) > 0
        for y in range(ny):
            ps = [full[0, z, y + 1, rows, :] for z in range(nz)]
            ns = [full[1, z, y + 1, rows, :] for z in range(nz)]
            for z in range(nz):
                row = y * nz + z
                p, n = ps[z], ns[z]
                u = jnp.where(rising_x, p, n)
                v = jnp.where(rising_x, n, p)
                u = jnp.where(first_lane, 0.0, pltpu.roll(u, 1, 1))
                v = jnp.where(last_lane, 0.0, pltpu.roll(v, nx - 1, 1))
                angular = turn[rows, row * nx : (row + 1) * nx]
                new_p = rest_speed * p + speed_x * jnp.where(rising_x, u, v) + angular
                new_n = rest_speed * n + speed_x * jnp.where(rising_x, v, u) + angular
                new_p = new_p + speed_y * jnp.where(
                    rising_y, full[0, z, y, rows, :], full[0, z, y + 2, rows, :]
                )
                new_n = new_n + speed_y * jnp.where(
                    rising_y, full[1, z, y + 2, rows, :], full[1, z, y, rows, :]
                )
                if z > 0:
                    new_p = new_p + speed_z * ps[z - 1]
                if z < nz - 1:
                    new_n = new_n + speed_z * ns[z + 1]
                if z < nz - 1:
                    new_rest[0, z, y, rows, :] = new_p
                else:
                    top = new_p
                if z > 0:
                    new_rest[1, z - 1, y, rows, :] = new_n
                else:
                    bottom = new_n
            piece, inner = divmod(part * 8, half // pieces)
            loads[2 * piece][y, pl.ds(inner, 8), :] = jnp.where(even, top, bottom)
            loads[2 * piece + 1][y, pl.ds(inner, 8), :] = jnp.where(even, bottom, top)


def close_body(plan, piece, table, even_ref, odd_ref, rest_ref, *refs):
    count = 1 + plan.z_two
    got, (field, held, sems) = refs[:count], refs[-3:]
    length = plan.half // PIECES
    offset = piece * length
    copies = field_copies(plan, held, field, sems, offset, length)
    even = is_even("gz")
    nz = plan.nz
    size = length // plan.chunks
    for chunk in range(plan.chunks):
        inner = pl.ds(chunk * size, size)
        start = offset + chunk * size
        rows = pl.ds(start, size)
        tab = table[rows, :]
        rising_z = column(tab, 6, (size, plan.nx)) > 0
        speed_z = column(tab, 3, (size, plan.nx))
        for y in range(plan.ny):
            arrived = [g[y, inner, :] for g in got]
            low = speed_z * from_below(even, arrived)
            high = speed_z * from_above(even, arrived)
            one, two = even_ref[y, rows, :], odd_ref[y, rows, :]
            for z in range(nz):
                if z == nz - 1:
                    p = jnp.where(even, one, two)
                else:
                    p = rest_ref[0, z, y, rows, :]
                if z == 0:
                    n = jnp.where(even, two, one)
                else:
                    n = rest_ref[1, z - 1, y, rows, :]
                if z == 0:
                    p = p + low
                if z == nz - 1:
                    n = n + high
                base = start * plan.rows + y * nz + z
                held[pl.ds(base, size, stride=plan.rows), :] = jnp.where(rising_z, p, n)
                base = base + plan.half * plan.rows
                held[pl.ds(base, size, stride=plan.rows), :] = jnp.where(rising_z, n, p)
        copies[2 * chunk].start()
        copies[2 * chunk + 1].start()
    for copy in copies:
        copy.wait()


def stay(value):
    return pltpu.with_memory_space_constraint(value, pltpu.HBM)


def call(body, outs, args, scratch=(), raw_in=(), raw_out=False, aliases=None):
    in_specs = []
    for i in range(len(args)):
        in_specs.append(pl.BlockSpec(memory_space=pltpu.HBM if i in raw_in else VMEM))
    moved = sum(math.prod(a.shape) * 4 for a in list(args) + list(outs))
    return pl.pallas_call(
        body,
        out_shape=outs,
        in_specs=in_specs,
        out_specs=[pl.BlockSpec(memory_space=pltpu.HBM if raw_out else VMEM)] * len(outs),
        scratch_shapes=list(scratch),
        input_output_aliases=aliases or {},
        cost_estimate=pl.CostEstimate(flops=8 * moved, bytes_accessed=moved, transcendentals=0),
        compiler_params=pltpu.CompilerParams(vmem_limit_bytes=32 << 20),
    )(*args)


def shards(fodf, directions, signs):
    plan = Plan(fodf.shape, lax.axis_size("gz"), lax.axis_size("gy"))
    half = plan.half
    field = fodf.reshape(plan.field.shape)
    edge_outs = [plan.edge] * (1 + plan.y_two)
    streamed = [
        VMEM(plan.field.shape, jnp.float32),
        pltpu.SemaphoreType.DMA((plan.chunks, 2)),
    ]
    state = call(
        functools.partial(send_body, plan),
        [plan.layer, plan.layer, plan.rest],
        [stay(signs), stay(field)],
        [VMEM(signs.shape, signs.dtype), *streamed, pltpu.SemaphoreType.DMA],
        raw_in=(0, 1),
    )
    signs, directions, *state = lax.optimization_barrier((signs, directions, *state))
    near = directions[:, :half]
    turn = signs[:, :half].astype(jnp.float32)
    speeds = TIME_STEP * jnp.abs(near)
    columns = jnp.concatenate(
        [1.0 - jnp.sum(speeds, 0, keepdims=True), speeds, turn[:2] * turn[2:], turn[2:]], 0
    )
    table = columns.T
    matrix = angular_matrix(near)
    *loads, rest = state
    got = []
    for step in range(ITERS):
        split_in = len(loads) // 2
        split_out = PIECES if step == ITERS - 2 else 1
        edges = call(
            functools.partial(edge_body, plan, step == 0, split_in),
            edge_outs,
            [table, *loads, rest, *got],
        )
        arriving = [
            exchange(loads[2 * piece], loads[2 * piece + 1], "gz") for piece in range(split_in)
        ]
        y_got = exchange(edges[0], edges[-1], "gy")
        load_outs = [plan.layer] * 2 if split_out == 1 else [plan.piece] * (2 * split_out)
        *loads, rest = call(
            functools.partial(step_body, plan, step == 0, split_in, split_out),
            [*load_outs, plan.rest],
            [table, matrix, *loads, rest, *got, *y_got],
            [
                VMEM((2, plan.nz, plan.ny + 2, half, plan.nx), jnp.float32),
                VMEM((half, plan.rows * plan.nx), jnp.bfloat16),
                VMEM((half, plan.rows * plan.nx), jnp.bfloat16),
                VMEM((half, plan.rows * plan.nx), jnp.float32),
            ],
        )
        got = arriving[0]
    written = []
    for piece in range(PIECES):
        args = [table, *loads, rest, *arriving[piece], *written]
        written = call(
            functools.partial(close_body, plan, piece),
            [plan.field],
            args,
            streamed,
            raw_in=(len(args) - 1,) if written else (),
            raw_out=True,
            aliases={len(args) - 1: 0} if written else None,
        )
    field = written[0]
    return field.reshape(fodf.shape)


def solution(mesh):
    placed = (P(None, "gy", "gz", None), P(), P())
    return jax.shard_map(
        shards, mesh=mesh, in_specs=placed, out_specs=P(None, "gy", "gz", None), check_vma=False
    )
```

```python
import functools
import math

import jax
import jax.numpy as jnp
from jax import lax
from jax.experimental import pallas as pl
from jax.experimental.pallas import tpu as pltpu
from jax.sharding import PartitionSpec as P


LMAX = 8
ITERS = 4
TIME_STEP = 0.5
DIFFUSION = 0.02

PIECES = 2
VMEM = pltpu.VMEM


def double_factorial(value):
    result = 1
    while value > 1:
        result = result * value
        value = value - 2
    return result


def harmonic_rows(directions):
    along_x, along_y, along_z = (directions[0], directions[1], directions[2])
    cosines = [jnp.ones_like(along_x)]
    sines = [jnp.zeros_like(along_x)]
    for _ in range(1, LMAX + 1):
        cosines.append(cosines[-1] * along_x - sines[-1] * along_y)
        sines.append(cosines[-2] * along_y + sines[-1] * along_x)
    legendre = {}
    for order in range(LMAX + 1):
        legendre[order, order] = double_factorial(2 * order - 1) * jnp.ones_like(along_z)
        if order + 1 <= LMAX:
            legendre[order + 1, order] = (2 * order + 1) * along_z * legendre[order, order]
        for degree in range(order + 2, LMAX + 1):
            legendre[degree, order] = (
                (2 * degree - 1) * along_z * legendre[degree - 1, order]
                - (degree + order - 1) * legendre[degree - 2, order]
            ) / (degree - order)
    basis_rows = []
    eigen_values = []
    for degree in range(0, LMAX + 1, 2):
        for order in range(degree + 1):
            weight_norm = math.sqrt(
                (2 * degree + 1) * math.factorial(degree - order) / math.factorial(degree + order)
            )
            basis_rows.append(weight_norm * legendre[degree, order] * cosines[order])
            eigen_values.append(-float(degree * (degree + 1)))
            if order > 0:
                basis_rows.append(weight_norm * legendre[degree, order] * sines[order])
                eigen_values.append(-float(degree * (degree + 1)))
    return (jnp.stack(basis_rows, 0), jnp.array(eigen_values, dtype=directions.dtype))


def angular_matrix(half):
    basis, eigen_values = harmonic_rows(half)
    gram = 2.0 * jnp.dot(basis, basis.T, precision=lax.Precision.HIGHEST)
    chol_lower = lax.linalg.cholesky(gram, symmetrize_input=False)
    scaled = (TIME_STEP * DIFFUSION * eigen_values)[:, None] * basis
    return call(
        functools.partial(solve_body, basis.shape[0]),
        [jax.ShapeDtypeStruct((basis.shape[1],) * 2, jnp.float32)],
        [padded(chol_lower), padded(scaled), padded(basis)],
    )[0]


def padded(value):
    return jnp.pad(value, ((0, -value.shape[0] % 8), (0, 0)))


def solve_body(count, chol, left, right, out):
    size, width = left.shape
    factor = chol[...]
    row = lax.broadcasted_iota(jnp.int32, factor.shape, 0)
    col = lax.broadcasted_iota(jnp.int32, factor.shape, 1)
    diagonal = jnp.where(row == col, factor, 0.0)
    by_lane = jnp.sum(diagonal, axis=0, keepdims=True)
    factor = jnp.where(row > col, factor / by_lane, 0.0)
    weight = jnp.sum(diagonal, axis=1, keepdims=True)
    weight = jnp.where(weight == 0.0, 1.0, weight)
    blocks = [
        [ref[8 * block : 8 * block + 8, :] for block in range(size // 8)] for ref in (left, right)
    ]
    for j in range(count):
        home, place = divmod(j, 8)
        pivots = [jnp.broadcast_to(side[home][place : place + 1, :], (8, width)) for side in blocks]
        for block in range(home, size // 8):
            ratio = jnp.broadcast_to(factor[8 * block : 8 * block + 8, j : j + 1], (8, width))
            for side, pivot in zip(blocks, pivots):
                side[block] = side[block] - ratio * pivot
    first, second = (jnp.concatenate(side, 0) for side in blocks)
    out[...] = lax.dot_general(
        first,
        second / (weight * weight),
        (((0,), (0,)), ((), ())),
        precision=lax.Precision.HIGHEST,
        preferred_element_type=jnp.float32,
    )


def exchange(even_load, odd_load, axis):
    peers = lax.axis_size(axis)
    first = [(i, i ^ 1) for i in range(peers)]
    second = [(i, i + 1 if i % 2 else i - 1) for i in range(1, peers - 1)]
    got = [lax.ppermute(even_load, axis, first)]
    if second:
        got.append(lax.ppermute(odd_load, axis, second))
    return got


class Plan:
    def __init__(self, shape, z_peers, y_peers):
        self.kk, self.ny, self.nz, self.nx = shape
        self.half = self.kk // 2
        self.rows = self.ny * self.nz
        self.chunks = 2
        cut = self.half * 2 // 3 // 16 * 16
        self.pieces = [
            jax.ShapeDtypeStruct((self.ny, size, self.nx), jnp.float32)
            for size in (cut, self.half - cut)
        ]
        self.z_two = z_peers > 2
        self.y_two = y_peers > 2
        self.layer = jax.ShapeDtypeStruct((self.ny, self.half, self.nx), jnp.float32)
        self.rest = jax.ShapeDtypeStruct((2, self.nz - 1, self.ny, self.half, self.nx), jnp.float32)
        self.edge = jax.ShapeDtypeStruct((self.nz, self.half, self.nx), jnp.float32)
        self.field = jax.ShapeDtypeStruct((self.kk * self.rows, self.nx), jnp.float32)


def is_even(axis):
    return lax.rem(lax.axis_index(axis), 2) == 0


def column(table, index, shape):
    return jnp.broadcast_to(table[:, index : index + 1], shape)


def from_below(even, got):
    first = got[0]
    if len(got) == 1:
        return jnp.where(even, jnp.zeros_like(first), first)
    return jnp.where(even, got[1], first)


def from_above(even, got):
    first = got[0]
    if len(got) == 1:
        return jnp.where(even, first, jnp.zeros_like(first))
    return jnp.where(even, first, got[1])


def write_edges(even, rising_y, get_p, get_n, plan, outs):
    for z in range(plan.nz):
        top, low = plan.ny - 1, 0
        up = jnp.where(rising_y, get_p(z, top), get_n(z, top))
        down = jnp.where(rising_y, get_n(z, low), get_p(z, low))
        outs[0][z] = jnp.where(even, up, down)
        if plan.y_two:
            outs[1][z] = jnp.where(even, down, up)


def row_to_column(row, size):
    square = jnp.broadcast_to(row, (size, size))
    same = lax.broadcasted_iota(jnp.int32, (size, size), 0) == lax.broadcasted_iota(
        jnp.int32, (size, size), 1
    )
    return jnp.sum(jnp.where(same, square, 0.0), axis=1, keepdims=True)


def field_copies(plan, source, target, sems, start=0, length=None):
    copies = []
    size = (length or plan.half) // plan.chunks
    depth = size * plan.rows
    for chunk in range(plan.chunks):
        for member in range(2):
            first = member * plan.half + start + chunk * size
            where = pl.ds(first * plan.rows, depth)
            copies.append(
                pltpu.make_async_copy(source.at[where], target.at[where], sems.at[chunk, member])
            )
    return copies


def load_pair(plan, held, start, size, row):
    pair = []
    for member in range(2):
        base = (member * plan.half + start) * plan.rows + row
        pair.append(held[pl.ds(base, size, stride=plan.rows), :])
    return pair


def send_body(plan, signs_raw, field_raw, even_ref, odd_ref, rest_ref, signs, field, sems, small):
    fetch = pltpu.make_async_copy(signs_raw, signs, small)
    fetch.start()
    copies = field_copies(plan, field_raw, field, sems)
    for copy in copies:
        copy.start()
    fetch.wait()
    even = is_even("gz")
    signs_z = signs[2:3, : plan.half].astype(jnp.float32)
    turn = jnp.broadcast_to(row_to_column(signs_z, plan.half), (plan.half, plan.nx))
    size = plan.half // plan.chunks
    for chunk in range(plan.chunks):
        copies[2 * chunk].wait()
        copies[2 * chunk + 1].wait()
        start = chunk * size
        rising_z = turn[start : start + size] > 0
        rows = pl.ds(start, size)
        for y in range(plan.ny):
            for z in range(plan.nz):
                a, b = load_pair(plan, field, start, size, y * plan.nz + z)
                p = jnp.where(rising_z, a, b)
                n = jnp.where(rising_z, b, a)
                if z < plan.nz - 1:
                    rest_ref[0, z, y, rows, :] = p
                else:
                    top = p
                if z > 0:
                    rest_ref[1, z - 1, y, rows, :] = n
                else:
                    bottom = n
            even_ref[y, rows, :] = jnp.where(even, top, bottom)
            odd_ref[y, rows, :] = jnp.where(even, bottom, top)


def state_refs(refs, pieces):
    loads, rest = refs[: 2 * pieces], refs[2 * pieces]
    return loads[0::2], loads[1::2], rest, refs[2 * pieces + 1 :]


def locate(refs, start):
    piece = 0
    while start >= refs[piece].shape[1]:
        start -= refs[piece].shape[1]
        piece += 1
    return piece, start


def take(refs, y, start, size):
    piece, inner = locate(refs, start)
    return refs[piece][y, pl.ds(inner, size), :]


def whole(refs, y):
    return jnp.concatenate([ref[y] for ref in refs], 0) if len(refs) > 1 else refs[0][y]


def member_reader(plan, even, state, got, speed_z):
    evens, odds, rest_ref = state

    def get_p(z, y):
        if z == plan.nz - 1:
            return jnp.where(even, whole(evens, y), whole(odds, y))
        value = rest_ref[0, z, y]
        if got is not None and z == 0:
            value = value + speed_z * from_below(even, [g[y] for g in got])
        return value

    def get_n(z, y):
        if z == 0:
            return jnp.where(even, whole(odds, y), whole(evens, y))
        value = rest_ref[1, z - 1, y]
        if got is not None and z == plan.nz - 1:
            value = value + speed_z * from_above(even, [g[y] for g in got])
        return value

    return get_p, get_n


def edge_body(plan, first, split_in, table, *refs):
    evens, odds, rest_ref, refs = state_refs(refs, split_in)
    count = 0 if first else 1 + plan.z_two
    got, edges = refs[:count] or None, refs[count:]
    shape = (plan.half, plan.nx)
    get_p, get_n = member_reader(
        plan, is_even("gz"), (evens, odds, rest_ref), got, column(table, 3, shape)
    )
    write_edges(is_even("gy"), column(table, 5, shape) > 0, get_p, get_n, plan, edges)


def split(value):
    high = value.astype(jnp.bfloat16)
    low = (value - high.astype(jnp.float32)).astype(jnp.bfloat16)
    return high, low


def step_body(plan, first, split_in, pieces, table, matrix, *refs):
    evens, odds, rest_ref, refs = state_refs(refs, split_in)
    z_count = 0 if first else 1 + plan.z_two
    y_count = 1 + plan.y_two
    got = None if first else refs[:z_count]
    y_got = refs[z_count : z_count + y_count]
    outs = refs[z_count + y_count :]
    loads, (new_rest, full, highs, lows, turn) = outs[: 2 * pieces], outs[2 * pieces :]
    half, nx, ny, nz = plan.half, plan.nx, plan.ny, plan.nz
    even = is_even("gz")
    y_even = is_even("gy")
    for part in range(half // 16):
        rows = pl.ds(part * 16, 16)
        speed_z = column(table[rows, :], 3, (16, nx))
        for z in range(nz):
            low = from_below(y_even, [g[z, rows, :] for g in y_got])
            high = from_above(y_even, [g[z, rows, :] for g in y_got])
            full[0, z, 0, rows, :] = low
            full[1, z, 0, rows, :] = low
            full[0, z, ny + 1, rows, :] = high
            full[1, z, ny + 1, rows, :] = high
        for y in range(ny):
            for z in range(nz):
                if z == nz - 1:
                    p = jnp.where(even, take(evens, y, part * 16, 16), take(odds, y, part * 16, 16))
                else:
                    p = rest_ref[0, z, y, rows, :]
                    if got is not None and z == 0:
                        p = p + speed_z * from_below(even, [g[y, rows, :] for g in got])
                if z == 0:
                    n = jnp.where(even, take(odds, y, part * 16, 16), take(evens, y, part * 16, 16))
                else:
                    n = rest_ref[1, z - 1, y, rows, :]
                    if got is not None and z == nz - 1:
                        n = n + speed_z * from_above(even, [g[y, rows, :] for g in got])
                full[0, z, y + 1, rows, :] = p
                full[1, z, y + 1, rows, :] = n
                row = y * nz + z
                high, low = split(p + n)
                highs[rows, row * nx : (row + 1) * nx] = high
                lows[rows, row * nx : (row + 1) * nx] = low
    m_high, m_low = split(matrix[...])
    width = nz * nx
    for y in range(ny):
        cols = slice(y * width, (y + 1) * width)
        high = highs[:, cols]
        turn[:, cols] = (
            jnp.dot(m_high, high, preferred_element_type=jnp.float32)
            + jnp.dot(m_low, high, preferred_element_type=jnp.float32)
            + jnp.dot(m_high, lows[:, cols], preferred_element_type=jnp.float32)
        )
    tile = (8, nx)
    lane = lax.broadcasted_iota(jnp.int32, tile, 1)
    first_lane = lane == 0
    last_lane = lane == nx - 1
    for part in range(half // 8):
        rows = pl.ds(part * 8, 8)
        tab = table[rows, :]
        rest_speed = column(tab, 0, tile)
        speed_x = column(tab, 1, tile)
        speed_y = column(tab, 2, tile)
        speed_z = column(tab, 3, tile)
        rising_x = column(tab, 4, tile) > 0
        rising_y = column(tab, 5, tile) > 0
        for y in range(ny):
            ps = [full[0, z, y + 1, rows, :] for z in range(nz)]
            ns = [full[1, z, y + 1, rows, :] for z in range(nz)]
            for z in range(nz):
                row = y * nz + z
                p, n = ps[z], ns[z]
                u = jnp.where(rising_x, p, n)
                v = jnp.where(rising_x, n, p)
                u = jnp.where(first_lane, 0.0, pltpu.roll(u, 1, 1))
                v = jnp.where(last_lane, 0.0, pltpu.roll(v, nx - 1, 1))
                angular = turn[rows, row * nx : (row + 1) * nx]
                new_p = rest_speed * p + speed_x * jnp.where(rising_x, u, v) + angular
                new_n = rest_speed * n + speed_x * jnp.where(rising_x, v, u) + angular
                new_p = new_p + speed_y * jnp.where(
                    rising_y, full[0, z, y, rows, :], full[0, z, y + 2, rows, :]
                )
                new_n = new_n + speed_y * jnp.where(
                    rising_y, full[1, z, y + 2, rows, :], full[1, z, y, rows, :]
                )
                if z > 0:
                    new_p = new_p + speed_z * ps[z - 1]
                if z < nz - 1:
                    new_n = new_n + speed_z * ns[z + 1]
                if z < nz - 1:
                    new_rest[0, z, y, rows, :] = new_p
                else:
                    top = new_p
                if z > 0:
                    new_rest[1, z - 1, y, rows, :] = new_n
                else:
                    bottom = new_n
            piece, inner = locate(loads[0::2], part * 8)
            loads[2 * piece][y, pl.ds(inner, 8), :] = jnp.where(even, top, bottom)
            loads[2 * piece + 1][y, pl.ds(inner, 8), :] = jnp.where(even, bottom, top)


def close_body(plan, piece, table, even_ref, odd_ref, rest_ref, *refs):
    count = 1 + plan.z_two
    got, (field, held, sems) = refs[:count], refs[-3:]
    length = plan.pieces[piece].shape[1]
    offset = sum(p.shape[1] for p in plan.pieces[:piece])
    copies = field_copies(plan, held, field, sems, offset, length)
    even = is_even("gz")
    nz = plan.nz
    size = length // plan.chunks
    for chunk in range(plan.chunks):
        inner = pl.ds(chunk * size, size)
        start = offset + chunk * size
        rows = pl.ds(start, size)
        tab = table[rows, :]
        rising_z = column(tab, 6, (size, plan.nx)) > 0
        speed_z = column(tab, 3, (size, plan.nx))
        for y in range(plan.ny):
            arrived = [g[y, inner, :] for g in got]
            low = speed_z * from_below(even, arrived)
            high = speed_z * from_above(even, arrived)
            one, two = even_ref[y, rows, :], odd_ref[y, rows, :]
            for z in range(nz):
                if z == nz - 1:
                    p = jnp.where(even, one, two)
                else:
                    p = rest_ref[0, z, y, rows, :]
                if z == 0:
                    n = jnp.where(even, two, one)
                else:
                    n = rest_ref[1, z - 1, y, rows, :]
                if z == 0:
                    p = p + low
                if z == nz - 1:
                    n = n + high
                base = start * plan.rows + y * nz + z
                held[pl.ds(base, size, stride=plan.rows), :] = jnp.where(rising_z, p, n)
                base = base + plan.half * plan.rows
                held[pl.ds(base, size, stride=plan.rows), :] = jnp.where(rising_z, n, p)
        copies[2 * chunk].start()
        copies[2 * chunk + 1].start()
    for copy in copies:
        copy.wait()


def stay(value):
    return pltpu.with_memory_space_constraint(value, pltpu.HBM)


def call(body, outs, args, scratch=(), raw_in=(), raw_out=False, aliases=None):
    in_specs = []
    for i in range(len(args)):
        in_specs.append(pl.BlockSpec(memory_space=pltpu.HBM if i in raw_in else VMEM))
    moved = sum(math.prod(a.shape) * 4 for a in list(args) + list(outs))
    return pl.pallas_call(
        body,
        out_shape=outs,
        in_specs=in_specs,
        out_specs=[pl.BlockSpec(memory_space=pltpu.HBM if raw_out else VMEM)] * len(outs),
        scratch_shapes=list(scratch),
        input_output_aliases=aliases or {},
        cost_estimate=pl.CostEstimate(flops=8 * moved, bytes_accessed=moved, transcendentals=0),
        compiler_params=pltpu.CompilerParams(vmem_limit_bytes=32 << 20),
    )(*args)


def shards(fodf, directions, signs):
    plan = Plan(fodf.shape, lax.axis_size("gz"), lax.axis_size("gy"))
    half = plan.half
    field = fodf.reshape(plan.field.shape)
    edge_outs = [plan.edge] * (1 + plan.y_two)
    streamed = [
        VMEM(plan.field.shape, jnp.float32),
        pltpu.SemaphoreType.DMA((plan.chunks, 2)),
    ]
    state = call(
        functools.partial(send_body, plan),
        [plan.layer, plan.layer, plan.rest],
        [stay(signs), stay(field)],
        [VMEM(signs.shape, signs.dtype), *streamed, pltpu.SemaphoreType.DMA],
        raw_in=(0, 1),
    )
    signs, directions, *state = lax.optimization_barrier((signs, directions, *state))
    near = directions[:, :half]
    turn = signs[:, :half].astype(jnp.float32)
    speeds = TIME_STEP * jnp.abs(near)
    columns = jnp.concatenate(
        [1.0 - jnp.sum(speeds, 0, keepdims=True), speeds, turn[:2] * turn[2:], turn[2:]], 0
    )
    table = columns.T
    matrix = angular_matrix(near)
    *loads, rest = state
    got = []
    for step in range(ITERS):
        split_in = len(loads) // 2
        split_out = PIECES if step == ITERS - 2 else 1
        edges = call(
            functools.partial(edge_body, plan, step == 0, split_in),
            edge_outs,
            [table, *loads, rest, *got],
        )
        arriving = [
            exchange(loads[2 * piece], loads[2 * piece + 1], "gz") for piece in range(split_in)
        ]
        y_got = exchange(edges[0], edges[-1], "gy")
        load_outs = [plan.layer] * 2 if split_out == 1 else [p for p in plan.pieces for _ in range(2)]
        *loads, rest = call(
            functools.partial(step_body, plan, step == 0, split_in, split_out),
            [*load_outs, plan.rest],
            [table, matrix, *loads, rest, *got, *y_got],
            [
                VMEM((2, plan.nz, plan.ny + 2, half, plan.nx), jnp.float32),
                VMEM((half, plan.rows * plan.nx), jnp.bfloat16),
                VMEM((half, plan.rows * plan.nx), jnp.bfloat16),
                VMEM((half, plan.rows * plan.nx), jnp.float32),
            ],
        )
        got = arriving[0]
    written = []
    for piece in range(PIECES):
        args = [table, *loads, rest, *arriving[piece], *written]
        written = call(
            functools.partial(close_body, plan, piece),
            [plan.field],
            args,
            streamed,
            raw_in=(len(args) - 1,) if written else (),
            raw_out=True,
            aliases={len(args) - 1: 0} if written else None,
        )
    field = written[0]
    return field.reshape(fodf.shape)


def solution(mesh):
    placed = (P(None, "gy", "gz", None), P(), P())
    return jax.shard_map(
        shards, mesh=mesh, in_specs=placed, out_specs=P(None, "gy", "gz", None), check_vma=False
    )
```
